32 devices in a mesh: ctx: 8 (over z, y), tp: 4 (over x, core).
Axes of the slice: x: 2, y: 2, z: 4, core: 2. Of those that a mesh axis runs over, the one named last changes fastest.
Arguments:
- projections: bfloat16 [3, 2048, 4096], P(None, 'ctx', 'tp'), may hold values from -6 to 6
- short_weights: float32 [3, 7, 4096], P(None, None, 'tp'), may hold values from -2 to 2
- skip_gain: float32 [4096], P('tp'), may hold values from -1 to 1
- filters: bfloat16 [256, 128], P('tp'), may hold values from -0.5 to 0.5
- out_weight: bfloat16 [4096, 4096], P('tp'), may hold values from -0.09375 to 0.09375
- out_cotangent: bfloat16 [2048, 4096], P(('ctx', 'tp')), may hold values from -6 to 6
Outputs:
- mixed: bfloat16 [2048, 4096], P(('ctx', 'tp'))
- proj_grad: float32 [3, 2048, 4096], P(None, 'ctx', 'tp')
- filter_grad: float32 [256, 128], P('tp', 'ctx')
The draws below stay inside these ranges and needn't reach their ends.
All inputs are finite; a program needn't handle non-finite values.
Results may differ from the reference program's by a relative error of at most 0.009.
Values may be sent and summed in bfloat16 or wider, within the bound.
No kernel may reach another device: no remote copies, remote signals or barrier semaphores. Data moves between devices by JAX's collectives and lax.ppermute only.
A program may use at most 128 MiB of HBM per device.

```python
import math
import jax
import jax.numpy as jnp
from jax import lax

D = 4096
D_OUT = 4096
GROUP = 16
FILT = 128
SHORT = 7
TOKENS = 2048
GROUPS = 256
N_TP = 4


def block_scale(own_key, extent, cuts, smallest, top_value):
    loudness, own = 1.0, jax.random.fold_in(own_key, 6)
    for position, blocks in cuts:
        steps = jnp.exp(jax.random.uniform(jax.random.fold_in(own, position), (blocks,), jnp.float32, smallest / len(cuts), top_value / len(cuts)))
        loudness = loudness * jnp.repeat(steps, extent[position] // blocks).reshape([-1 if axis == position else 1 for axis in range(len(extent))])
    return loudness


def scatter_about(own_key, extent, width, reach, cuts=(), kind=jnp.bfloat16):
    array = width * jax.random.normal(own_key, extent, jnp.float32)
    if cuts:
        array = array * block_scale(own_key, extent, cuts, -0.22, 0.18)
    return jnp.clip(array, -reach, reach).astype(kind)


def setup_inputs(seed: int = 0) -> dict:
    splits = jax.random.split(jax.random.key(seed), 7)
    projections = scatter_about(splits[0], (3, TOKENS, D), 1.0, 6.0, ((1, 8), (2, 4)))
    short_weights = scatter_about(splits[1], (3, SHORT, D), SHORT ** -0.5, 2.0, ((2, 4),), jnp.float32)
    skip_gain = jnp.clip(jax.random.uniform(splits[2], (D,), jnp.float32, -1.0, 1.0) * block_scale(splits[2], (D,), ((0, 4),), -0.4, 0.0), -1.0, 1.0)
    filters = scatter_about(splits[3], (GROUPS, FILT), FILT ** -0.5, 0.5, ((0, 4),))
    out_weight = scatter_about(splits[4], (D, D_OUT), D ** -0.5, 0.09375, ((0, 4),))
    out_cotangent = scatter_about(splits[5], (TOKENS, D_OUT), 1.0, 6.0, ((0, 32),))
    return {"projections": projections, "short_weights": short_weights, "skip_gain": skip_gain, "filters": filters, "out_weight": out_weight, "out_cotangent": out_cotangent}


def lag_table(filters, row_count, col_count, lag_shift, direction):
    taps_long = filters.shape[1]
    offset = direction * (jnp.arange(col_count, dtype=jnp.int32)[None, :] - jnp.arange(row_count, dtype=jnp.int32)[:, None]) + lag_shift
    inside = (offset >= 0) & (offset < taps_long)
    picked = jnp.take(filters, jnp.clip(offset, 0, taps_long - 1), axis=1)
    return jnp.where(inside[None, :, :], picked, jnp.zeros_like(picked))

def short_apply(extended, weights, out_rows):
    short_taps = weights.shape[1]
    running = jnp.zeros((extended.shape[0], out_rows, extended.shape[2]), jnp.float32)
    for tap_index in range(short_taps):
        first_row = short_taps - 1 - tap_index
        running = running + weights[:, tap_index, None, :] * extended[:, first_row:first_row + out_rows, :].astype(jnp.float32)
    return running

def block_conv(extended, table, group_count):
    taps_long = table.shape[1]
    block_count = extended.shape[0] // taps_long - 1
    blocks = extended.astype(jnp.float32).reshape(block_count + 1, taps_long, group_count, -1)
    table_wide = table.astype(jnp.float32)
    lower = jnp.einsum('gir,brgk->bigk', table_wide[:, :, :taps_long], blocks[:-1], precision=lax.Precision.HIGHEST)
    upper = jnp.einsum('gir,brgk->bigk', table_wide[:, :, taps_long:], blocks[1:], precision=lax.Precision.HIGHEST)
    return (lower + upper).reshape(block_count * taps_long, -1)

def lag_products(grad_rows, extended, group_count, taps_long):
    block_count = grad_rows.shape[0] // taps_long
    grad_blocks = grad_rows.astype(jnp.float32).reshape(block_count, taps_long, group_count, -1)
    source = extended.astype(jnp.float32).reshape(block_count + 1, taps_long, group_count, -1)
    lower = jnp.einsum('bigk,brgk->gir', grad_blocks, source[:-1], precision=lax.Precision.HIGHEST)
    upper = jnp.einsum('bigk,brgk->gir', grad_blocks, source[1:], precision=lax.Precision.HIGHEST)
    scores = jnp.concatenate([lower, upper], axis=2)
    shifted = jnp.concatenate([scores[:, :, 1:], jnp.zeros((group_count, taps_long, 1), jnp.float32)], axis=2)
    flat = shifted.reshape(group_count, 2 * taps_long * taps_long)
    flat = jnp.concatenate([flat, jnp.zeros((group_count, taps_long), jnp.float32)], axis=1)
    skewed = flat.reshape(group_count, taps_long, 2 * taps_long + 1)[:, :, :taps_long]
    return lax.optimization_barrier(jnp.sum(skewed, axis=1))[:, ::-1]

def reference(projections, short_weights, skip_gain, filters, out_weight, out_cotangent):
    short_edge = SHORT - 1
    padded = jnp.concatenate([jnp.zeros((3, short_edge, D), jnp.bfloat16), projections], axis=1)
    features = short_apply(padded, short_weights, TOKENS)
    gated_prod = (features[1] * features[2]).astype(jnp.bfloat16)
    fwd_ext = jnp.concatenate([jnp.zeros((FILT, D), jnp.bfloat16), gated_prod], axis=0)
    long_out = block_conv(fwd_ext, lag_table(filters, FILT, 2 * FILT, FILT, -1), GROUPS) + skip_gain * gated_prod.astype(jnp.float32)
    mixer_out = (features[0] * long_out).astype(jnp.bfloat16)
    weight_wide = out_weight.astype(jnp.float32)
    mixer_wide = mixer_out.astype(jnp.float32)
    block_width = D // N_TP

    def block_partial(total, block_index):
        start = (block_index * block_width).astype(jnp.int32)
        columns = lax.dynamic_slice_in_dim(mixer_wide, start, block_width, 1)
        rows = lax.dynamic_slice_in_dim(weight_wide, start, block_width, 0)
        term = jnp.dot(columns, rows, precision=lax.Precision.HIGHEST).astype(jnp.bfloat16)
        term = lax.optimization_barrier(term)
        return (total + term.astype(jnp.float32), None)
    summed, unused = lax.scan(block_partial, jnp.zeros((TOKENS, D_OUT), jnp.float32), jnp.arange(N_TP, dtype=jnp.int32))
    mixed = summed.astype(jnp.bfloat16)
    mixer_grad = jnp.dot(out_cotangent.astype(jnp.float32), weight_wide.T, precision=lax.Precision.HIGHEST)
    query_grad = mixer_grad * long_out
    long_grad = (mixer_grad * features[0]).astype(jnp.bfloat16)
    back_ext = jnp.concatenate([long_grad, jnp.zeros((FILT, D), jnp.bfloat16)], axis=0)
    back_conv = block_conv(back_ext, lag_table(filters, FILT, 2 * FILT, 0, 1), GROUPS)
    gated_grad = back_conv + skip_gain * long_grad.astype(jnp.float32)
    feature_grads = jnp.stack([query_grad, gated_grad * features[2], gated_grad * features[1]])
    grad_ext = jnp.concatenate([feature_grads, jnp.zeros((3, short_edge, D), jnp.float32)], axis=1)
    proj_grad = jnp.zeros((3, TOKENS, D), jnp.float32)
    for tap_index in range(SHORT):
        proj_grad = proj_grad + short_weights[:, tap_index, None, :] * grad_ext[:, tap_index:tap_index + TOKENS, :]
    lag_grads = lag_products(long_grad, fwd_ext, GROUPS, FILT)
    filter_grad = lag_grads / math.sqrt(TOKENS * GROUP)
    return (mixed, proj_grad, filter_grad)
```

```python
import math

import jax
import jax.numpy as jnp
from jax import lax
from jax.experimental import pallas as pl
from jax.experimental.pallas import tpu as pltpu
from jax.sharding import PartitionSpec as P

LANES = 128
SIDE = 256
EDGE = 8
BF = jnp.bfloat16
F32 = jnp.float32
NT = (((1,), (1,)), ((), ()))
TN = (((0,), (0,)), ((), ()))


def params(mib=56):
    return pltpu.CompilerParams(vmem_limit_bytes=mib << 20)


def cost(flops, moved):
    return pl.CostEstimate(flops=int(flops), transcendentals=0, bytes_accessed=int(moved))


def exchanged(value, axis, bit):
    count = lax.axis_size(axis)
    return lax.ppermute(value, axis, [(index, index ^ bit) for index in range(count)])


def passed_along(value, axis, steps):
    count = lax.axis_size(axis)
    initial, last = (max(0, -steps), min(count, count - steps))
    return lax.ppermute(value, axis, [(source, source + steps) for source in range(initial, last)])


def iota(shape, dim):
    return lax.broadcasted_iota(jnp.int32, shape, dim)


def flip_matrix(taps, total, dtype):
    rows, cols = iota((taps, taps), 0), iota((taps, taps), 1)
    return ((rows + cols) % taps == total).astype(F32).astype(dtype)


def skewed(row, height):
    wide = jnp.broadcast_to(row, (height, row.shape[1]))
    return pltpu.roll(wide, 0, 1, stride=1, stride_axis=0)


def group_of_lane(shape, width):
    return (iota(shape, 1) % LANES) // width


def picked(stacked, rows, per, width):
    owner = group_of_lane((rows, stacked.shape[1]), width)
    total = stacked[:rows]
    for member in range(1, per):
        total = jnp.where(owner == member, stacked[member * rows : (member + 1) * rows], total)
    return total


def side_by_side(ext, blocks):
    return jnp.concatenate(
        [ext[block * LANES : (block + 2) * LANES] for block in range(blocks)], axis=1
    )


def short_sum(ref, base, step, weights, rows):
    total = weights[0:1] * ref[pl.ds(base, rows), :]
    for tap in range(1, weights.shape[0]):
        total = total + weights[tap : tap + 1] * ref[pl.ds(base + step * tap, rows), :]
    return total


def tail_kernel(proj_ref, sw_ref, out_ref, xs_ref):
    rows = proj_ref.shape[1]
    taps = out_ref.shape[0] - 4 * EDGE
    reach = taps + 16
    for half in range(proj_ref.shape[2] // LANES):
        lanes = pl.ds(half * LANES, LANES)
        for part in range(1, 3):
            xs_ref[part, pl.ds(0, reach), :] = proj_ref[part, pl.ds(rows - reach, reach), lanes].astype(F32)
        feats = [short_sum(xs_ref.at[part], 16, -1, sw_ref[part, :, lanes], taps) for part in (1, 2)]
        out_ref[pl.ds(0, taps), lanes] = (feats[0] * feats[1]).astype(BF)
        ends = [proj_ref[part, pl.ds(rows - 16, 16), lanes].astype(F32)[16 - EDGE :] for part in range(3)]
        out_ref[pl.ds(taps, 4 * EDGE), lanes] = jnp.concatenate(
            ends + [jnp.zeros((EDGE, LANES), F32)], axis=0
        ).astype(BF)


def gated_tail(projections, short_weights, taps):
    _, rows, channels = projections.shape
    reach = taps + 4 * EDGE
    return pl.pallas_call(
        tail_kernel,
        name="gated_tail",
        grid=(channels // SIDE,),
        in_specs=[
            pl.BlockSpec((3, rows, SIDE), lambda n: (0, 0, n)),
            pl.BlockSpec((3, short_weights.shape[1], SIDE), lambda n: (0, 0, n)),
        ],
        out_specs=pl.BlockSpec((reach, SIDE), lambda n: (0, n)),
        out_shape=jax.ShapeDtypeStruct((reach, channels), BF),
        scratch_shapes=[pltpu.VMEM((3, taps + 16, LANES), F32)],
        compiler_params=params(),
        cost_estimate=cost(4 * taps * channels * 7, 4 * rows * channels * 2),
    )(projections, short_weights)


def forward_kernel(
    proj_ref, halo_ref, sw_ref, skip_ref, filt_ref, w_ref,
    feat_ref, long_ref, gext_ref, *rest,
):
    term_refs, (xs_ref, mix_ref, wv_ref, sem) = rest[:-4], rest[-4:]
    step, steps = pl.program_id(0), pl.num_programs(0)
    rows, side = proj_ref.shape[1], proj_ref.shape[2]
    taps = filt_ref.shape[1]
    per = filt_ref.shape[0] * LANES // side
    width = LANES // per
    blocks = rows // taps
    fetch = pltpu.make_async_copy(w_ref, wv_ref, sem)

    @pl.when(step == 0)
    def _():
        fetch.start()

    turned = jnp.dot(filt_ref[...], flip_matrix(taps, 0, BF), preferred_element_type=F32)
    shape = (taps, taps)
    inside = iota(shape, 1) <= iota(shape, 0)
    for half in range(side // LANES):
        lanes = pl.ds(half * LANES, LANES)
        ends = halo_ref[pl.ds(taps, 4 * EDGE), lanes].astype(F32)
        feats = []
        for part in range(3):
            xs_ref[part, pl.ds(0, EDGE), :] = ends[part * EDGE : (part + 1) * EDGE]
            xs_ref[part, pl.ds(EDGE, rows), :] = proj_ref[part, :, lanes].astype(F32)
            feats.append(short_sum(xs_ref.at[part], EDGE, -1, sw_ref[part, :, lanes], rows))
            feat_ref[part, :, lanes] = feats[part]
        gated = (feats[1] * feats[2]).astype(BF)
        ext = jnp.concatenate([halo_ref[pl.ds(0, taps), lanes], gated], axis=0)
        gext_ref[:, lanes] = ext
        tables = []
        for member in range(per):
            index = half * per + member
            turn = skewed(turned[index : index + 1], taps)
            tables.append(
                jnp.concatenate(
                    [jnp.where(inside, 0.0, turn), jnp.where(inside, turn, 0.0)], axis=1
                ).astype(BF)
            )
        stacked = jnp.dot(
            jnp.concatenate(tables, axis=0), side_by_side(ext, blocks), preferred_element_type=F32
        )
        conv = picked(stacked, taps, per, width)
        conv = jnp.concatenate(
            [conv[:, block * LANES : (block + 1) * LANES] for block in range(blocks)], axis=0
        )
        long_out = conv + skip_ref[:, lanes] * gated.astype(F32)
        long_ref[:, lanes] = long_out
        mix_ref[:, pl.ds(pl.multiple_of(step * side + half * LANES, LANES), LANES)] = (
            feats[0] * long_out
        ).astype(BF)

    @pl.when(step == steps - 1)
    def _():
        me = lax.axis_index("tp")
        count = len(term_refs)
        own = rows // count
        ordered = jnp.concatenate(
            [mix_ref[pl.ds(pl.multiple_of((me ^ k) * own, own), own), :] for k in range(count)], axis=0
        )
        fetch.wait()
        chunk = 512
        for start in range(0, wv_ref.shape[1], chunk):
            cols = pl.ds(start, chunk)
            terms = jnp.dot(ordered, wv_ref[:, cols], preferred_element_type=F32).astype(BF)
            for k in range(count):
                term_refs[k][:, cols] = terms[k * own : (k + 1) * own]


def forward(projections, halo, short_weights, skip, filters, out_weight, n_tp):
    _, rows, channels = projections.shape
    taps = filters.shape[1]
    features = out_weight.shape[1]
    groups = filters.shape[0] * SIDE // channels
    own = rows // n_tp
    return pl.pallas_call(
        forward_kernel,
        name="forward",
        grid=(channels // SIDE,),
        in_specs=[
            pl.BlockSpec((3, rows, SIDE), lambda n: (0, 0, n)),
            pl.BlockSpec((halo.shape[0], SIDE), lambda n: (0, n)),
            pl.BlockSpec((3, short_weights.shape[1], SIDE), lambda n: (0, 0, n)),
            pl.BlockSpec((1, SIDE), lambda n: (0, n)),
            pl.BlockSpec((groups, taps), lambda n: (n, 0)),
            pl.BlockSpec(memory_space=pl.ANY),
        ],
        out_specs=[
            pl.BlockSpec((3, rows, SIDE), lambda n: (0, 0, n)),
            pl.BlockSpec((rows, SIDE), lambda n: (0, n)),
            pl.BlockSpec((rows + taps, SIDE), lambda n: (0, n)),
        ]
        + [pl.BlockSpec((own, features), lambda n: (0, 0))] * n_tp,
        out_shape=[
            jax.ShapeDtypeStruct((3, rows, channels), F32),
            jax.ShapeDtypeStruct((rows, channels), F32),
            jax.ShapeDtypeStruct((rows + taps, channels), BF),
        ]
        + [jax.ShapeDtypeStruct((own, features), BF)] * n_tp,
        scratch_shapes=[
            pltpu.VMEM((3, rows + EDGE, LANES), F32),
            pltpu.VMEM((rows, channels), BF),
            pltpu.VMEM((channels, features), BF),
            pltpu.SemaphoreType.DMA,
        ],
        compiler_params=params(),
        cost_estimate=cost(2 * rows * channels * (features + 2048), (channels + rows) * features * 2 + rows * channels * 24),
    )(projections, halo, short_weights, skip, filters, out_weight)


def backward_kernel(n_tp, n_ctx, *refs):
    pieces, refs = refs[:n_tp], refs[n_tp:]
    (w_ref, feat_ref, long_ref, gext_ref, skip_ref, filt_ref,
     lgrad_ref, qgrad_ref, head_ref, lag_ref, cot_ref, lags_ref, turn_ref, sems) = refs
    step, steps = pl.program_id(0), pl.num_programs(0)
    rows, side = lgrad_ref.shape
    taps = filt_ref.shape[1]
    per = filt_ref.shape[0] * LANES // side
    width = LANES // per
    blocks = rows // taps
    own = rows // n_tp

    @pl.when(step == 0)
    def _():
        me = lax.axis_index("tp")
        copies = [
            pltpu.make_async_copy(
                pieces[k], cot_ref.at[pl.ds(pl.multiple_of((me ^ k) * own, own), own), :], sems.at[k]
            )
            for k in range(n_tp)
        ]
        for copy in copies:
            copy.start()
        for copy in copies:
            copy.wait()

    grads = lax.dot_general(cot_ref[...], w_ref[...], NT, preferred_element_type=F32)
    taps_f = filt_ref[...].astype(F32)
    top = (EDGE, taps)
    later = iota(top, 1) >= iota(top, 0)
    square = (taps, taps)
    inside = iota(square, 1) + iota(square, 0) < taps
    reverse = flip_matrix(taps, taps - 1, BF)
    sums = []
    for half in range(side // LANES):
        lanes = pl.ds(half * LANES, LANES)
        grad = grads[:, half * LANES : (half + 1) * LANES]
        query = grad * long_ref[:, lanes]
        qgrad_ref[:, lanes] = query
        lgrad = (grad * feat_ref[0, :, lanes]).astype(BF)
        lgrad_ref[:, lanes] = lgrad
        tables = []
        for member in range(per):
            index = half * per + member
            turn = skewed(taps_f[index : index + 1], EDGE)
            tables.append(
                jnp.concatenate(
                    [jnp.where(later, turn, 0.0), jnp.where(later, 0.0, turn)], axis=1
                )
            )
        stacked = jnp.dot(
            jnp.concatenate(tables, axis=0).astype(BF), lgrad[: 2 * taps], preferred_element_type=F32
        )
        gated_grad = picked(stacked, EDGE, per, width) + skip_ref[:, lanes] * lgrad[:16].astype(F32)[:EDGE]
        head_ref[pl.ds(0, taps), lanes] = lgrad[:taps]
        head_ref[pl.ds(taps, 4 * EDGE), lanes] = jnp.concatenate(
            [
                query[:EDGE],
                gated_grad * feat_ref[2, pl.ds(0, EDGE), lanes],
                gated_grad * feat_ref[1, pl.ds(0, EDGE), lanes],
                jnp.zeros((EDGE, LANES), F32),
            ],
            axis=0,
        ).astype(BF)
        wide = jnp.concatenate(
            [lgrad[block * taps : (block + 1) * taps] for block in range(blocks)], axis=1
        )
        wide = jnp.dot(reverse, wide, preferred_element_type=F32).astype(BF)
        owner = group_of_lane((1, wide.shape[1]), width)
        left = jnp.concatenate(
            [wide * (owner == member).astype(F32).astype(BF) for member in range(per)], axis=0
        )
        scores = lax.dot_general(
            left, side_by_side(gext_ref[:, lanes], blocks), NT, preferred_element_type=F32
        )
        for member in range(per):
            block = scores[member * taps : (member + 1) * taps]
            merged = jnp.where(inside, block[:, taps:], block[:, :taps])
            merged = pltpu.roll(merged, 0, 1, stride=1, stride_axis=0)
            sums.append(jnp.sum(merged, axis=0, keepdims=True))
    lags_ref[pl.ds(pl.multiple_of(step * len(sums), len(sums)), len(sums)), :] = jnp.concatenate(sums, axis=0)

    @pl.when(step == steps - 1)
    def _():
        turned = lax.dot_general(
            flip_matrix(taps, taps - 1, F32), lags_ref[...], NT,
            precision=lax.Precision.HIGHEST, preferred_element_type=F32,
        )
        share = taps // n_ctx
        if share % EDGE:
            lag_ref[...] = turned
            return
        turn_ref[...] = turned
        here = lax.axis_index("ctx")
        for k in range(n_ctx):
            lag_ref[pl.ds(k * share, share), :] = turn_ref[
                pl.ds(pl.multiple_of((here ^ k) * share, share), share), :
            ]


def backward(pieces, out_weight, feats, long_out, gext, skip, filters, n_ctx):
    n_tp = len(pieces)
    rows, channels = long_out.shape
    taps = filters.shape[1]
    features = out_weight.shape[1]
    groups = filters.shape[0] * SIDE // channels
    reach = taps + 4 * EDGE
    return pl.pallas_call(
        lambda *refs: backward_kernel(n_tp, n_ctx, *refs),
        name="backward",
        grid=(channels // SIDE,),
        in_specs=[pl.BlockSpec(memory_space=pl.ANY)] * n_tp
        + [
            pl.BlockSpec((SIDE, features), lambda n: (n, 0)),
            pl.BlockSpec((3, rows, SIDE), lambda n: (0, 0, n)),
            pl.BlockSpec((rows, SIDE), lambda n: (0, n)),
            pl.BlockSpec((rows + taps, SIDE), lambda n: (0, n)),
            pl.BlockSpec((1, SIDE), lambda n: (0, n)),
            pl.BlockSpec((groups, taps), lambda n: (n, 0)),
        ],
        out_specs=[
            pl.BlockSpec((rows, SIDE), lambda n: (0, n)),
            pl.BlockSpec((rows, SIDE), lambda n: (0, n)),
            pl.BlockSpec((reach, SIDE), lambda n: (0, n)),
            pl.BlockSpec((taps, filters.shape[0]), lambda n: (0, 0)),
        ],
        out_shape=[
            jax.ShapeDtypeStruct((rows, channels), BF),
            jax.ShapeDtypeStruct((rows, channels), F32),
            jax.ShapeDtypeStruct((reach, channels), BF),
            jax.ShapeDtypeStruct((taps, filters.shape[0]), F32),
        ],
        scratch_shapes=[
            pltpu.VMEM((rows, features), BF),
            pltpu.VMEM((filters.shape[0], taps), F32),
            pltpu.VMEM((taps, filters.shape[0]), F32),
            pltpu.SemaphoreType.DMA((n_tp,)),
        ],
        compiler_params=params(),
        cost_estimate=cost(2 * rows * channels * (features + 2048), (channels + rows) * features * 2 + rows * channels * 24),
    )(*pieces, out_weight, feats, long_out, gext, skip, filters)


def last_kernel(lgrad_ref, head_ref, qgrad_ref, feat_ref, sw_ref, skip_ref, filt_ref, out_ref, fg_ref):
    rows, side = lgrad_ref.shape
    taps = filt_ref.shape[1]
    per = filt_ref.shape[0] * LANES // side
    width = LANES // per
    blocks = rows // taps
    taps_f = filt_ref[...].astype(F32)
    square = (taps, taps)
    later = iota(square, 1) >= iota(square, 0)
    for half in range(side // LANES):
        lanes = pl.ds(half * LANES, LANES)
        lgrad = lgrad_ref[:, lanes]
        ext = jnp.concatenate([lgrad, head_ref[pl.ds(0, taps), lanes]], axis=0)
        tables = []
        for member in range(per):
            index = half * per + member
            turn = skewed(taps_f[index : index + 1], taps)
            tables.append(
                jnp.concatenate(
                    [jnp.where(later, turn, 0.0), jnp.where(later, 0.0, turn)], axis=1
                ).astype(BF)
            )
        stacked = jnp.dot(
            jnp.concatenate(tables, axis=0), side_by_side(ext, blocks), preferred_element_type=F32
        )
        conv = picked(stacked, taps, per, width)
        conv = jnp.concatenate(
            [conv[:, block * LANES : (block + 1) * LANES] for block in range(blocks)], axis=0
        )
        gated_grad = conv + skip_ref[:, lanes] * lgrad.astype(F32)
        heads = head_ref[pl.ds(taps, 4 * EDGE), lanes].astype(F32)
        fg_ref[0, pl.ds(0, rows), :] = qgrad_ref[:, lanes]
        fg_ref[1, pl.ds(0, rows), :] = gated_grad * feat_ref[2, :, lanes]
        fg_ref[2, pl.ds(0, rows), :] = gated_grad * feat_ref[1, :, lanes]
        for part in range(3):
            fg_ref[part, pl.ds(rows, EDGE), :] = heads[part * EDGE : (part + 1) * EDGE]
            out_ref[part, :, lanes] = short_sum(fg_ref.at[part], 0, 1, sw_ref[part, :, lanes], rows)


def last(lgrad, heads, qgrad, feats, short_weights, skip, filters):
    rows, channels = lgrad.shape
    taps = filters.shape[1]
    groups = filters.shape[0] * SIDE // channels
    return pl.pallas_call(
        last_kernel,
        name="last",
        grid=(channels // SIDE,),
        in_specs=[
            pl.BlockSpec((rows, SIDE), lambda n: (0, n)),
            pl.BlockSpec((heads.shape[0], SIDE), lambda n: (0, n)),
            pl.BlockSpec((rows, SIDE), lambda n: (0, n)),
            pl.BlockSpec((3, rows, SIDE), lambda n: (0, 0, n)),
            pl.BlockSpec((3, short_weights.shape[1], SIDE), lambda n: (0, 0, n)),
            pl.BlockSpec((1, SIDE), lambda n: (0, n)),
            pl.BlockSpec((groups, taps), lambda n: (n, 0)),
        ],
        out_specs=pl.BlockSpec((3, rows, SIDE), lambda n: (0, 0, n)),
        out_shape=jax.ShapeDtypeStruct((3, rows, channels), F32),
        scratch_shapes=[pltpu.VMEM((3, rows + EDGE, LANES), F32)],
        compiler_params=params(),
        cost_estimate=cost(2 * rows * channels * 2048, rows * channels * 34),
    )(lgrad, heads, qgrad, feats, short_weights, skip, filters)


def bits_of(count):
    return [1 << position for position in range(count.bit_length() - 1)]


def shards(projections, short_weights, skip_gain, filters, out_weight, out_cotangent):
    _, rows, channels = projections.shape
    group_count, taps = filters.shape
    n_tp, n_ctx = lax.axis_size("tp"), lax.axis_size("ctx")
    skip = skip_gain.reshape(1, channels)

    pieces = {0: out_cotangent}
    for bit in reversed(bits_of(n_tp)):
        pieces.update({k | bit: exchanged(piece, "tp", bit) for k, piece in list(pieces.items())})
    pieces = [pieces[k] for k in range(n_tp)]

    halo = passed_along(gated_tail(projections, short_weights, taps), "ctx", 1)
    feats, long_out, gext, *terms = forward(
        projections, halo, short_weights, skip, filters, out_weight, n_tp
    )
    lgrad, qgrad, heads, lags = backward(
        pieces, out_weight, feats, long_out, gext, skip, filters, n_ctx
    )
    later = passed_along(heads, "ctx", -1)

    for bit in bits_of(n_tp):
        arrived = {k: exchanged(terms[k].astype(BF), "tp", bit) for k in reversed(range(0, n_tp, bit)) if k & bit}
        for k, term in arrived.items():
            terms[k ^ bit] = terms[k ^ bit].astype(F32) + term.astype(F32)
    mixed = terms[0].astype(BF)

    proj_grad = last(lgrad, later, qgrad, feats, short_weights, skip, filters)

    norm_factor = 1.0 / math.sqrt(rows * n_ctx * (channels // group_count))
    share = taps // n_ctx
    if share % EDGE:
        lags = lax.psum_scatter(lags, "ctx", scatter_dimension=0, tiled=True)
    else:
        for bit in reversed(bits_of(n_ctx)):
            lags = lags[: bit * share] + exchanged(lags[bit * share :], "ctx", bit)
    filter_grad = lags.T * norm_factor
    return (mixed, proj_grad, filter_grad)


def solution(mesh):
    placed = (
        P(None, "ctx", "tp"),
        P(None, None, "tp"),
        P("tp"),
        P("tp", None),
        P("tp", None),
        P(("ctx", "tp"), None),
    )
    return jax.shard_map(
        shards,
        mesh=mesh,
        in_specs=placed,
        out_specs=(P(("ctx", "tp"), None), P(None, "ctx", "tp"), P("tp", "ctx")),
        check_vma=False,
    )
```

```python
import math

import jax
import jax.numpy as jnp
from jax import lax
from jax.experimental import pallas as pl
from jax.experimental.pallas import tpu as pltpu
from jax.sharding import PartitionSpec as P

LANES = 128
SIDE = 256
EDGE = 8
COVER = 10**11
BF = jnp.bfloat16
F32 = jnp.float32
NT = (((1,), (1,)), ((), ()))
TN = (((0,), (0,)), ((), ()))


def called(kernel, name, operands, results, scratch=(), kept=(), cover=1, mib=16):
    spaces = [
        pltpu.HBM if position in kept else pltpu.VMEM
        for position in range(len(operands) + len(results))
    ]
    first = len(operands)
    placed = [
        pltpu.with_memory_space_constraint(value, space) for value, space in zip(operands, spaces)
    ]
    return pl.pallas_call(
        kernel,
        name=name,
        in_specs=[pl.BlockSpec(memory_space=space) for space in spaces[:first]],
        out_specs=[pl.BlockSpec(memory_space=space) for space in spaces[first:]],
        out_shape=[space(*result) for space, result in zip(spaces[first:], results)],
        scratch_shapes=list(scratch),
        compiler_params=pltpu.CompilerParams(vmem_limit_bytes=mib << 20),
        cost_estimate=pl.CostEstimate(flops=cover, transcendentals=0, bytes_accessed=1),
    )(*placed)


def repeated(count, body):
    def step(index, carry):
        body(index)
        return carry

    lax.fori_loop(0, count, step, 0)


def unrolled(count, body):
    for index in range(count):
        body(index)


def multiple(value, of):
    return value if isinstance(value, int) else pl.multiple_of(value, of)


def lanes_of(block, half):
    return pl.ds(multiple(block * SIDE + half * LANES, LANES), LANES)


def rows_of(block, size):
    return pl.ds(multiple(block * size, size), size)


def exchanged(value, axis, bit):
    count = lax.axis_size(axis)
    return lax.ppermute(value, axis, [(index, index ^ bit) for index in range(count)])


def passed_along(value, axis, steps):
    count = lax.axis_size(axis)
    initial, last = (max(0, -steps), min(count, count - steps))
    return lax.ppermute(value, axis, [(source, source + steps) for source in range(initial, last)])


def iota(shape, dim):
    return lax.broadcasted_iota(jnp.int32, shape, dim)


def flip_matrix(taps, total, dtype):
    rows, cols = iota((taps, taps), 0), iota((taps, taps), 1)
    return ((rows + cols) % taps == total).astype(F32).astype(dtype)


def skewed(row, height):
    wide = jnp.broadcast_to(row, (height, row.shape[1]))
    return pltpu.roll(wide, 0, 1, stride=1, stride_axis=0)


def group_of_lane(shape, width):
    return (iota(shape, 1) % LANES) // width


def picked(stacked, rows, per, width):
    owner = group_of_lane((rows, stacked.shape[1]), width)
    total = stacked[:rows]
    for member in range(1, per):
        total = jnp.where(owner == member, stacked[member * rows : (member + 1) * rows], total)
    return total


def side_by_side(ext, blocks):
    return jnp.concatenate(
        [ext[block * LANES : (block + 2) * LANES] for block in range(blocks)], axis=1
    )


def short_sum(ref, base, step, weights, rows):
    total = weights[0:1] * ref[pl.ds(base, rows), :]
    for tap in range(1, weights.shape[0]):
        total = total + weights[tap : tap + 1] * ref[pl.ds(base + step * tap, rows), :]
    return total


def tail_kernel(proj_hbm, sw_hbm, out_ref, proj_ref, sw_ref, xs_ref, sems):
    rows, channels = proj_hbm.shape[1:]
    taps = out_ref.shape[0] - 4 * EDGE
    reach = taps + 16
    copies = [
        pltpu.make_async_copy(sw_hbm, sw_ref, sems.at[0]),
        pltpu.make_async_copy(proj_hbm.at[:, pl.ds(rows - reach, reach), :], proj_ref, sems.at[1]),
    ]
    for copy in copies:
        copy.start()
    for copy in copies:
        copy.wait()

    def body(block):
        for half in range(SIDE // LANES):
            lanes = lanes_of(block, half)
            for part in range(1, 3):
                xs_ref[half, part] = proj_ref[part, :, lanes].astype(F32)
            feats = [
                short_sum(xs_ref.at[half, part], 16, -1, sw_ref[part, :, lanes], taps) for part in (1, 2)
            ]
            out_ref[pl.ds(0, taps), lanes] = (feats[0] * feats[1]).astype(BF)
            ends = [proj_ref[part, pl.ds(taps, 16), lanes].astype(F32)[16 - EDGE :] for part in range(3)]
            out_ref[pl.ds(taps, 4 * EDGE), lanes] = jnp.concatenate(
                ends + [jnp.zeros((EDGE, LANES), F32)], axis=0
            ).astype(BF)

    unrolled(channels // SIDE, body)


def gated_tail(projections, short_weights, taps):
    _, rows, channels = projections.shape
    return called(
        tail_kernel, "gated_tail", (projections, short_weights),
        [((taps + 4 * EDGE, channels), BF)],
        scratch=[
            pltpu.VMEM((3, taps + 16, channels), BF),
            pltpu.VMEM(short_weights.shape, F32),
            pltpu.VMEM((2, 3, taps + 16, LANES), F32),
            pltpu.SemaphoreType.DMA((2,)),
        ],
        kept=(0, 1),
    )[0]


def prepare_kernel(
    proj_hbm, sw_hbm, filt_hbm, w_hbm, skip_hbm, after_hbm,
    feat_ref, edge_ref, gated_ref, fwd_ref, bwd_ref, sw_ref, skip_ref, w_ref,
    proj_ref, filt_ref, xs_ref, sems,
):
    rows, channels = proj_ref.shape[1:]
    groups, taps = filt_ref.shape
    per = groups * SIDE // channels
    copies = [
        pltpu.make_async_copy(source, target, sems.at[index])
        for index, (source, target) in enumerate(
            (
                (filt_hbm, filt_ref), (proj_hbm, proj_ref), (sw_hbm, sw_ref), (skip_hbm, skip_ref),
                (w_hbm, w_ref),
            )
        )
    ]
    for copy in copies:
        copy.start()
    shape = (taps, taps)
    inside = iota(shape, 1) <= iota(shape, 0)
    later = iota(shape, 1) >= iota(shape, 0)
    copies[0].wait()

    def build(block):
        plain = filt_ref[rows_of(block, per), :]
        turned = jnp.dot(plain, flip_matrix(taps, 0, BF), preferred_element_type=F32)
        plain = plain.astype(F32)
        for member in range(per):
            place = pl.ds(multiple((block * per + member) * taps, taps), taps)
            turn = skewed(turned[member : member + 1], taps)
            fwd_ref[place, pl.ds(0, taps)] = jnp.where(inside, 0.0, turn).astype(BF)
            fwd_ref[place, pl.ds(taps, taps)] = jnp.where(inside, turn, 0.0).astype(BF)
            turn = skewed(plain[member : member + 1], taps)
            bwd_ref[place, pl.ds(0, taps)] = jnp.where(later, turn, 0.0).astype(BF)
            bwd_ref[place, pl.ds(taps, taps)] = jnp.where(later, 0.0, turn).astype(BF)

    repeated(channels // SIDE, build)
    for copy in copies[1:4]:
        copy.wait()

    def features(block):
        for half in range(SIDE // LANES):
            lanes = lanes_of(block, half)
            feats = []
            for part in range(3):
                xs = xs_ref.at[half, part]
                xs[pl.ds(0, EDGE), :] = jnp.zeros((EDGE, LANES), F32)
                full = proj_ref[part, :, lanes].astype(F32)
                xs[pl.ds(EDGE, rows), :] = full
                edge_ref[part, :, lanes] = full[:EDGE]
                feats.append(short_sum(xs, EDGE, -1, sw_ref[part, :, lanes], rows))
                feat_ref[part, :, lanes] = feats[part]
            gated_ref[:, lanes] = (feats[1] * feats[2]).astype(BF)

    repeated(channels // SIDE, features)
    copies[4].wait()


def prepare(projections, short_weights, filters, out_weight, skip, after):
    _, rows, channels = projections.shape
    groups, taps = filters.shape
    return called(
        prepare_kernel, "prepare", (projections, short_weights, filters, out_weight, skip, after),
        [
            ((3, rows, channels), F32),
            ((3, EDGE, channels), F32),
            ((rows, channels), BF),
            ((groups * taps, 2 * taps), BF),
            ((groups * taps, 2 * taps), BF),
            (short_weights.shape, F32),
            (skip.shape, F32),
            (out_weight.shape, BF),
        ],
        scratch=[
            pltpu.VMEM(projections.shape, BF),
            pltpu.VMEM(filters.shape, BF),
            pltpu.VMEM((2, 3, rows + EDGE, LANES), F32),
            pltpu.SemaphoreType.DMA((5,)),
        ],
        kept=(0, 1, 2, 3, 4),
        cover=COVER,
    )


def block_conv(table, ext, taps, per, width):
    blocks = ext.shape[0] // taps - 1
    stacked = jnp.dot(table, side_by_side(ext, blocks), preferred_element_type=F32)
    conv = picked(stacked, taps, per, width)
    return jnp.concatenate(
        [conv[:, block * LANES : (block + 1) * LANES] for block in range(blocks)], axis=0
    )


def halving_order(count):
    order = [0]
    for bit in reversed(bits_of(count)):
        order = order + [index | bit for index in order]
    return order


def forward_kernel(
    feat_ref, edge_ref, gated_ref, halo_ref, sw_ref, skip_ref, table_ref,
    first_ref, long_ref, gext_ref, mix_ref, xs_ref,
):
    rows, channels = gated_ref.shape
    taps = table_ref.shape[1] // 2
    per = table_ref.shape[0] // taps * LANES // channels
    width = LANES // per

    def body(block):
        for half in range(SIDE // LANES):
            lanes = lanes_of(block, half)
            ends = halo_ref[pl.ds(taps, 4 * EDGE), lanes].astype(F32)
            firsts = []
            for part in range(3):
                xs = xs_ref.at[half, part]
                xs[pl.ds(0, EDGE), :] = ends[part * EDGE : (part + 1) * EDGE]
                xs[pl.ds(EDGE, EDGE), :] = edge_ref[part, :, lanes]
                firsts.append(short_sum(xs, EDGE, -1, sw_ref[part, :, lanes], EDGE))
                first_ref[part, :, lanes] = firsts[part]
            begun = jnp.concatenate(
                [firsts[1] * firsts[2], gated_ref[pl.ds(0, 16), lanes].astype(F32)[EDGE:]], axis=0
            ).astype(BF)
            gext_ref[pl.ds(0, taps), lanes] = halo_ref[pl.ds(0, taps), lanes]
            gext_ref[pl.ds(taps, 16), lanes] = begun
            gext_ref[pl.ds(taps + 16, rows - 16), lanes] = gated_ref[pl.ds(16, rows - 16), lanes]
            ext = gext_ref[:, lanes]
            table = table_ref[rows_of(block * 2 + half, per * taps), :]
            long_out = block_conv(table, ext, taps, per, width) + skip_ref[:, lanes] * ext[taps:].astype(F32)
            long_ref[:, lanes] = long_out
            query = jnp.concatenate([firsts[0], feat_ref[0, pl.ds(EDGE, rows - EDGE), lanes]], axis=0)
            mix_ref[:, lanes] = (query * long_out).astype(BF)

    unrolled(channels // SIDE, body)


def forward(feats, edges, gated, halo, short_weights, skip, table):
    _, rows, channels = feats.shape
    taps = table.shape[1] // 2
    return called(
        forward_kernel, "forward", (feats, edges, gated, halo, short_weights, skip, table),
        [
            ((3, EDGE, channels), F32),
            ((rows, channels), F32),
            ((rows + taps, channels), BF),
            ((rows, channels), BF),
        ],
        scratch=[pltpu.VMEM((2, 3, 2 * EDGE, LANES), F32)],
        cover=COVER,
    )


def project_kernel(own, mix_ref, w_ref, *refs):
    term_refs = refs[-2:]
    rows = mix_ref.shape[0]
    me = lax.axis_index("tp")
    order = halving_order(rows // own)
    ordered = jnp.concatenate([mix_ref[rows_of(me ^ k, own), :] for k in order], axis=0)
    kept = term_refs[0].shape[0]
    chunk = 512

    def project(block):
        cols = pl.ds(multiple(block * chunk, chunk), chunk)
        terms = jnp.dot(ordered, w_ref[:, cols], preferred_element_type=F32).astype(BF)
        term_refs[0][:, cols] = terms[:kept]
        if kept < rows:
            term_refs[1][:, cols] = terms[kept:]

    repeated(w_ref.shape[1] // chunk, project)


def project(mixer_out, out_weight, after, n_tp):
    rows, features = mixer_out.shape[0], out_weight.shape[1]
    own = rows // n_tp
    split = [rows // 2] * 2 if n_tp > 1 else [rows]
    return called(
        lambda *refs: project_kernel(own, *refs), "project", (mixer_out, out_weight, *after),
        [((size, features), BF) for size in split],
    )


def grads_kernel(n_tp, *refs):
    pieces, (w_ref, grad_ref, cot_ref) = refs[:n_tp], refs[n_tp:]
    rows, channels = grad_ref.shape
    own = rows // n_tp
    me = lax.axis_index("tp")
    for k in range(n_tp):
        cot_ref[rows_of(me ^ k, own), :] = pieces[k][...]

    def body(block):
        place = rows_of(block, SIDE)
        grad_ref[:, place] = lax.dot_general(
            cot_ref[...], w_ref[place, :], NT, preferred_element_type=F32
        )

    unrolled(channels // SIDE, body)


def mixer_grads(pieces, out_weight):
    n_tp = len(pieces)
    channels, features = out_weight.shape
    rows = pieces[0].shape[0] * n_tp
    return called(
        lambda *refs: grads_kernel(n_tp, *refs), "grads", (*pieces, out_weight),
        [((rows, channels), F32)],
        scratch=[pltpu.VMEM((rows, features), BF)],
    )[0]


def backward_kernel(
    grad_ref, feat_ref, first_ref, long_ref, skip_ref, table_ref, lgrad_ref, qgrad_ref, head_ref
):
    rows, channels = lgrad_ref.shape
    taps = table_ref.shape[1] // 2
    groups = table_ref.shape[0] // taps
    per = groups * LANES // channels
    width = LANES // per

    def body(block):
        for half in range(SIDE // LANES):
            lanes = lanes_of(block, half)
            grad = grad_ref[:, lanes]
            query = grad * long_ref[:, lanes]
            qgrad_ref[:, lanes] = query
            feat = jnp.concatenate(
                [first_ref[0, :, lanes], feat_ref[0, pl.ds(EDGE, rows - EDGE), lanes]], axis=0
            )
            lgrad = (grad * feat).astype(BF)
            lgrad_ref[:, lanes] = lgrad
            first = multiple((block * 2 + half) * per * taps, taps)
            top = jnp.concatenate(
                [table_ref[pl.ds(first + member * taps, 16), :] for member in range(per)], axis=0
            )
            stacked = jnp.dot(top, lgrad[: 2 * taps], preferred_element_type=F32)
            gated_grad = picked(stacked, 16, per, width) + skip_ref[:, lanes] * lgrad[:16].astype(F32)
            head_ref[pl.ds(0, taps), lanes] = lgrad[:taps]
            head_ref[pl.ds(taps, 4 * EDGE), lanes] = jnp.concatenate(
                [
                    query[:EDGE],
                    gated_grad[:EDGE] * first_ref[2, :, lanes],
                    gated_grad[:EDGE] * first_ref[1, :, lanes],
                    jnp.zeros((EDGE, LANES), F32),
                ],
                axis=0,
            ).astype(BF)

    unrolled(channels // SIDE, body)


def backward(grads, feats, firsts, long_out, skip, table):
    rows, channels = long_out.shape
    taps = table.shape[1] // 2
    return called(
        backward_kernel, "backward", (grads, feats, firsts, long_out, skip, table),
        [((rows, channels), BF), ((rows, channels), F32), ((taps + 4 * EDGE, channels), BF)],
    )


def lag_kernel(count, lgrad_ref, gext_ref, after_ref, lag_ref, lags_ref, turn_ref):
    rows, channels = lgrad_ref.shape
    groups, taps = lags_ref.shape
    per = groups * LANES // channels
    width = LANES // per
    blocks = rows // taps
    square = (taps, taps)
    inside = iota(square, 1) + iota(square, 0) < taps
    reverse = flip_matrix(taps, taps - 1, BF)

    def body(block):
        sums = []
        for half in range(SIDE // LANES):
            lanes = lanes_of(block, half)
            wide = jnp.concatenate(
                [lgrad_ref[pl.ds(part * taps, taps), lanes] for part in range(blocks)], axis=1
            )
            wide = jnp.dot(reverse, wide, preferred_element_type=F32).astype(BF)
            owner = group_of_lane((1, wide.shape[1]), width)
            left = jnp.concatenate(
                [wide * (owner == member).astype(F32).astype(BF) for member in range(per)], axis=0
            )
            scores = lax.dot_general(
                left, side_by_side(gext_ref[:, lanes], blocks), NT, preferred_element_type=F32
            )
            for member in range(per):
                score = scores[member * taps : (member + 1) * taps]
                merged = jnp.where(inside, score[:, taps:], score[:, :taps])
                merged = pltpu.roll(merged, 0, 1, stride=1, stride_axis=0)
                sums.append(jnp.sum(merged, axis=0, keepdims=True))
        lags_ref[rows_of(block, len(sums)), :] = jnp.concatenate(sums, axis=0)

    unrolled(channels // SIDE, body)
    turn_ref[...] = lax.dot_general(
        flip_matrix(taps, taps - 1, F32), lags_ref[...], NT,
        precision=lax.Precision.HIGHEST, preferred_element_type=F32,
    )
    if count == 1:
        lag_ref[...] = turn_ref[...]
        return
    here, share = lax.axis_index("ctx"), taps // count
    for k in range(count):
        lag_ref[pl.ds(k * share, share), :] = turn_ref[rows_of(here ^ k, share), :]


def lag_sums(lgrad, gext, groups, count, after):
    rows, channels = lgrad.shape
    taps = gext.shape[0] - rows
    return called(
        lambda *refs: lag_kernel(count, *refs), "lag_sums", (lgrad, gext, after),
        [((taps, groups), F32)],
        scratch=[pltpu.VMEM((groups, taps), F32), pltpu.VMEM((taps, groups), F32)],
    )[0]


def feature_kernel(lgrad_ref, head_ref, qgrad_ref, feat_ref, first_ref, skip_ref, table_ref, fg_ref):
    rows, channels = lgrad_ref.shape
    taps = table_ref.shape[1] // 2
    per = table_ref.shape[0] // taps * LANES // channels
    width = LANES // per
    rest = pl.ds(EDGE, rows - EDGE)

    def body(block):
        for half in range(SIDE // LANES):
            lanes = lanes_of(block, half)
            lgrad = lgrad_ref[:, lanes]
            ext = jnp.concatenate([lgrad, head_ref[pl.ds(0, taps), lanes]], axis=0)
            table = table_ref[rows_of(block * 2 + half, per * taps), :]
            gated_grad = block_conv(table, ext, taps, per, width) + skip_ref[:, lanes] * lgrad.astype(F32)
            heads = head_ref[pl.ds(taps, 4 * EDGE), lanes].astype(F32)
            for part in range(3):
                fg = fg_ref.at[block * 2 + half, part]
                if part:
                    fg[pl.ds(0, EDGE), :] = gated_grad[:EDGE] * first_ref[3 - part, :, lanes]
                    fg[rest, :] = gated_grad[EDGE:] * feat_ref[3 - part, rest, lanes]
                else:
                    fg[pl.ds(0, rows), :] = qgrad_ref[:, lanes]
                fg[pl.ds(rows, EDGE), :] = heads[part * EDGE : (part + 1) * EDGE]

    unrolled(channels // SIDE, body)


def feature_grads(lgrad, heads, qgrad, feats, firsts, skip, table):
    rows, channels = lgrad.shape
    return called(
        feature_kernel, "feature_grads", (lgrad, heads, qgrad, feats, firsts, skip, table),
        [((channels // LANES, 3, rows + EDGE, LANES), F32)],
    )[0]


def short_grads_kernel(fg_ref, sw_ref, out_ref, res_ref, sems):
    rows, channels = out_ref.shape[1:]

    def copy_of(block):
        lanes = pl.ds(multiple(block * SIDE, SIDE), SIDE)
        return pltpu.make_async_copy(res_ref.at[:, :, lanes], out_ref.at[:, :, lanes], sems.at[block])

    def body(block):
        for half in range(SIDE // LANES):
            lanes = lanes_of(block, half)
            for part in range(3):
                fg = fg_ref.at[block * 2 + half, part]
                res_ref[part, :, lanes] = short_sum(fg, 0, 1, sw_ref[part, :, lanes], rows)
        copy_of(block).start()

    unrolled(channels // SIDE, body)
    for block in range(channels // SIDE):
        copy_of(block).wait()


def short_grads(fgs, short_weights):
    blocks, _, rows, _ = fgs.shape
    rows, channels = rows - EDGE, blocks * LANES
    return called(
        short_grads_kernel, "short_grads", (fgs, short_weights),
        [((3, rows, channels), F32)],
        scratch=[
            pltpu.VMEM((3, rows, channels), F32),
            pltpu.SemaphoreType.DMA((channels // SIDE,)),
        ],
        kept=(2,),
    )[0]


def last_kernel(factor, term_ref, final_ref, lag_ref, arrived_ref, mixed_hbm, filter_hbm, mixed_ref, filter_ref, sems):
    own = mixed_ref.shape[0]
    mixed = term_ref[pl.ds(0, own), :].astype(F32)
    if final_ref.shape[0] == own:
        mixed = mixed + final_ref[...].astype(F32)
    mixed_ref[...] = mixed.astype(BF)
    total = lag_ref[pl.ds(0, filter_ref.shape[0]), :]
    if arrived_ref.shape == filter_ref.shape:
        total = total + arrived_ref[...]
    filter_ref[...] = total * factor
    copies = [
        pltpu.make_async_copy(mixed_ref, mixed_hbm, sems.at[0]),
        pltpu.make_async_copy(filter_ref, filter_hbm, sems.at[1]),
    ]
    for copy in copies:
        copy.start()
    for copy in copies:
        copy.wait()


def last(terms, final, lags, arrived, own, share, factor):
    results = [((own, terms.shape[1]), BF), ((share, lags.shape[1]), F32)]
    return called(
        lambda *refs: last_kernel(factor, *refs), "last", (terms, final, lags, arrived), results,
        scratch=[pltpu.VMEM(*result) for result in results] + [pltpu.SemaphoreType.DMA((2,))],
        kept=(4, 5),
    )


def bits_of(count):
    return [1 << position for position in range(count.bit_length() - 1)]


def shards(projections, short_weights, skip_gain, filters, out_weight, out_cotangent):
    _, rows, channels = projections.shape
    group_count, taps = filters.shape
    n_tp, n_ctx = lax.axis_size("tp"), lax.axis_size("ctx")
    skip = skip_gain.reshape(1, channels)

    pack = gated_tail(projections, short_weights, taps)
    halo = passed_along(pack, "ctx", 1)

    feats, edges, gated, fwd_table, bwd_table, weights, skip, out_weight = prepare(
        projections, short_weights, filters, out_weight, skip, pack
    )
    pieces = {0: out_cotangent}
    for bit in reversed(bits_of(n_tp)):
        pieces.update({k | bit: exchanged(piece, "tp", bit) for k, piece in list(pieces.items())})
    pieces = [pieces[k] for k in range(n_tp)]

    firsts, long_out, gext, mixer_out = forward(feats, edges, gated, halo, weights, skip, fwd_table)
    terms = project(mixer_out, out_weight, pieces[1::2], n_tp)
    grads = mixer_grads(pieces, out_weight)
    lgrad, qgrad, heads = backward(grads, feats, firsts, long_out, skip, bwd_table)
    later = passed_along(heads, "ctx", -1)

    own = rows // n_tp
    held = after = final = terms[0]
    sent = terms[-1]
    for bit in bits_of(n_tp):
        arrived = exchanged(sent, "tp", bit)
        if bit == 1:
            arrived, lgrad = lax.optimization_barrier((arrived, lgrad))
        if 2 * bit == n_tp:
            final = arrived
            break
        held = held.astype(F32) + arrived.astype(F32)
        half = held.shape[0] // 2
        sent = after = held[half:].astype(BF)
        held = held[:half]

    share = taps // n_ctx
    apart = share % EDGE == 0
    lags = lag_sums(lgrad, gext, group_count, n_ctx if apart else 1, after)
    fgs = feature_grads(lgrad, later, qgrad, feats, firsts, skip, bwd_table)
    proj_grad = short_grads(fgs, weights)
    arrived = lags
    for position, bit in enumerate(reversed(bits_of(n_ctx)) if apart else ()):
        if position:
            lags = lags[: bit * share * 2] + arrived
        arrived = exchanged(lags[bit * share :], "ctx", bit)
        if position == 0:
            arrived, later = lax.optimization_barrier((arrived, later))
        if position == 1:
            arrived, final = lax.optimization_barrier((arrived, final))
    if not apart:
        lags = arrived = lax.psum_scatter(lags, "ctx", scatter_dimension=0, tiled=True)
    factor = 1.0 / math.sqrt(rows * n_ctx * (channels // group_count))
    if not apart:
        arrived = final
    mixed, filter_grad = last(held, final, lags, arrived, own, share, factor)
    filter_grad = filter_grad.T
    return (mixed, proj_grad, filter_grad)


def solution(mesh):
    placed = (
        P(None, "ctx", "tp"),
        P(None, None, "tp"),
        P("tp"),
        P("tp", None),
        P("tp", None),
        P(("ctx", "tp"), None),
    )
    return jax.shard_map(
        shards,
        mesh=mesh,
        in_specs=placed,
        out_specs=(P(("ctx", "tp"), None), P(None, "ctx", "tp"), P("tp", "ctx")),
        check_vma=False,
    )
```

```python
import math

import jax
import jax.numpy as jnp
from jax import lax
from jax.experimental import pallas as pl
from jax.experimental.pallas import tpu as pltpu
from jax.sharding import PartitionSpec as P

LANES = 128
SIDE = 256
EDGE = 8
COVER = 10**11
BF = jnp.bfloat16
F32 = jnp.float32
NT = (((1,), (1,)), ((), ()))
TN = (((0,), (0,)), ((), ()))


def called(kernel, name, operands, results, scratch=(), kept=(), cover=1, mib=16):
    spaces = [
        pltpu.HBM if position in kept else pltpu.VMEM
        for position in range(len(operands) + len(results))
    ]
    first = len(operands)
    placed = [
        pltpu.with_memory_space_constraint(value, space) for value, space in zip(operands, spaces)
    ]
    return pl.pallas_call(
        kernel,
        name=name,
        in_specs=[pl.BlockSpec(memory_space=space) for space in spaces[:first]],
        out_specs=[pl.BlockSpec(memory_space=space) for space in spaces[first:]],
        out_shape=[space(*result) for space, result in zip(spaces[first:], results)],
        scratch_shapes=list(scratch),
        compiler_params=pltpu.CompilerParams(vmem_limit_bytes=mib << 20),
        cost_estimate=pl.CostEstimate(flops=cover, transcendentals=0, bytes_accessed=1),
    )(*placed)


def repeated(count, body):
    def step(index, carry):
        body(index)
        return carry

    lax.fori_loop(0, count, step, 0)


def unrolled(count, body):
    for index in range(count):
        body(index)


def multiple(value, of):
    return value if isinstance(value, int) else pl.multiple_of(value, of)


def lanes_of(block, half):
    return pl.ds(multiple(block * SIDE + half * LANES, LANES), LANES)


def rows_of(block, size):
    return pl.ds(multiple(block * size, size), size)


def exchanged(value, axis, bit):
    count = lax.axis_size(axis)
    return lax.ppermute(value, axis, [(index, index ^ bit) for index in range(count)])


def passed_along(value, axis, steps):
    count = lax.axis_size(axis)
    initial, last = (max(0, -steps), min(count, count - steps))
    return lax.ppermute(value, axis, [(source, source + steps) for source in range(initial, last)])


def iota(shape, dim):
    return lax.broadcasted_iota(jnp.int32, shape, dim)


def flip_matrix(taps, total, dtype):
    rows, cols = iota((taps, taps), 0), iota((taps, taps), 1)
    return ((rows + cols) % taps == total).astype(F32).astype(dtype)


def skewed(row, height):
    wide = jnp.broadcast_to(row, (height, row.shape[1]))
    return pltpu.roll(wide, 0, 1, stride=1, stride_axis=0)


def group_of_lane(shape, width):
    return (iota(shape, 1) % LANES) // width


def picked(stacked, rows, per, width):
    owner = group_of_lane((rows, stacked.shape[1]), width)
    total = stacked[:rows]
    for member in range(1, per):
        total = jnp.where(owner == member, stacked[member * rows : (member + 1) * rows], total)
    return total


def side_by_side(ext, blocks):
    return jnp.concatenate(
        [ext[block * LANES : (block + 2) * LANES] for block in range(blocks)], axis=1
    )


def short_sum(ref, base, step, weights, rows):
    total = weights[0:1] * ref[pl.ds(base, rows), :]
    for tap in range(1, weights.shape[0]):
        total = total + weights[tap : tap + 1] * ref[pl.ds(base + step * tap, rows), :]
    return total


def tail_kernel(proj_hbm, sw_hbm, out_ref, proj_ref, sw_ref, xs_ref, sems):
    rows, channels = proj_hbm.shape[1:]
    taps = out_ref.shape[0] - 4 * EDGE
    reach = taps + 16
    copies = [
        pltpu.make_async_copy(sw_hbm, sw_ref, sems.at[0]),
        pltpu.make_async_copy(proj_hbm.at[:, pl.ds(rows - reach, reach), :], proj_ref, sems.at[1]),
    ]
    for copy in copies:
        copy.start()
    for copy in copies:
        copy.wait()

    def body(block):
        for half in range(SIDE // LANES):
            lanes = lanes_of(block, half)
            for part in range(1, 3):
                xs_ref[half, part] = proj_ref[part, :, lanes].astype(F32)
            feats = [
                short_sum(xs_ref.at[half, part], 16, -1, sw_ref[part, :, lanes], taps) for part in (1, 2)
            ]
            out_ref[pl.ds(0, taps), lanes] = (feats[0] * feats[1]).astype(BF)
            ends = [proj_ref[part, pl.ds(taps, 16), lanes].astype(F32)[16 - EDGE :] for part in range(3)]
            out_ref[pl.ds(taps, 4 * EDGE), lanes] = jnp.concatenate(
                ends + [jnp.zeros((EDGE, LANES), F32)], axis=0
            ).astype(BF)

    unrolled(channels // SIDE, body)


def gated_tail(projections, short_weights, taps):
    _, rows, channels = projections.shape
    return called(
        tail_kernel, "gated_tail", (projections, short_weights),
        [((taps + 4 * EDGE, channels), BF)],
        scratch=[
            pltpu.VMEM((3, taps + 16, channels), BF),
            pltpu.VMEM(short_weights.shape, F32),
            pltpu.VMEM((2, 3, taps + 16, LANES), F32),
            pltpu.SemaphoreType.DMA((2,)),
        ],
        kept=(0, 1),
    )[0]


def prepare_kernel(
    proj_hbm, sw_hbm, filt_hbm, w_hbm, skip_hbm, after_hbm,
    feat_ref, edge_ref, gated_ref, fwd_ref, bwd_ref, sw_ref, skip_ref, w_ref,
    proj_ref, filt_ref, xs_ref, sems,
):
    rows, channels = proj_ref.shape[1:]
    groups, taps = filt_ref.shape
    per = groups * SIDE // channels
    copies = [
        pltpu.make_async_copy(source, target, sems.at[index])
        for index, (source, target) in enumerate(
            (
                (filt_hbm, filt_ref), (proj_hbm, proj_ref), (sw_hbm, sw_ref), (skip_hbm, skip_ref),
                (w_hbm, w_ref),
            )
        )
    ]
    for copy in copies:
        copy.start()
    shape = (taps, taps)
    inside = iota(shape, 1) <= iota(shape, 0)
    later = iota(shape, 1) >= iota(shape, 0)
    copies[0].wait()

    def build(block):
        plain = filt_ref[rows_of(block, per), :]
        turned = jnp.dot(plain, flip_matrix(taps, 0, BF), preferred_element_type=F32)
        plain = plain.astype(F32)
        for member in range(per):
            place = pl.ds(multiple((block * per + member) * taps, taps), taps)
            turn = skewed(turned[member : member + 1], taps)
            fwd_ref[place, pl.ds(0, taps)] = jnp.where(inside, 0.0, turn).astype(BF)
            fwd_ref[place, pl.ds(taps, taps)] = jnp.where(inside, turn, 0.0).astype(BF)
            turn = skewed(plain[member : member + 1], taps)
            bwd_ref[place, pl.ds(0, taps)] = jnp.where(later, turn, 0.0).astype(BF)
            bwd_ref[place, pl.ds(taps, taps)] = jnp.where(later, 0.0, turn).astype(BF)

    repeated(channels // SIDE, build)
    for copy in copies[1:4]:
        copy.wait()

    def features(block):
        for half in range(SIDE // LANES):
            lanes = lanes_of(block, half)
            feats = []
            for part in range(3):
                xs = xs_ref.at[half, part]
                xs[pl.ds(0, EDGE), :] = jnp.zeros((EDGE, LANES), F32)
                full = proj_ref[part, :, lanes].astype(F32)
                xs[pl.ds(EDGE, rows), :] = full
                edge_ref[part, :, lanes] = full[:EDGE]
                feats.append(short_sum(xs, EDGE, -1, sw_ref[part, :, lanes], rows))
                feat_ref[part, :, lanes] = feats[part]
            gated_ref[:, lanes] = (feats[1] * feats[2]).astype(BF)

    repeated(channels // SIDE, features)
    copies[4].wait()


def prepare(projections, short_weights, filters, out_weight, skip, after):
    _, rows, channels = projections.shape
    groups, taps = filters.shape
    return called(
        prepare_kernel, "prepare", (projections, short_weights, filters, out_weight, skip, after),
        [
            ((3, rows, channels), F32),
            ((3, EDGE, channels), F32),
            ((rows, channels), BF),
            ((groups * taps, 2 * taps), BF),
            ((groups * taps, 2 * taps), BF),
            (short_weights.shape, F32),
            (skip.shape, F32),
            (out_weight.shape, BF),
        ],
        scratch=[
            pltpu.VMEM(projections.shape, BF),
            pltpu.VMEM(filters.shape, BF),
            pltpu.VMEM((2, 3, rows + EDGE, LANES), F32),
            pltpu.SemaphoreType.DMA((5,)),
        ],
        kept=(0, 1, 2, 3, 4),
        cover=COVER,
    )


def block_conv(table, ext, taps, per, width):
    blocks = ext.shape[0] // taps - 1
    stacked = jnp.dot(table, side_by_side(ext, blocks), preferred_element_type=F32)
    conv = picked(stacked, taps, per, width)
    return jnp.concatenate(
        [conv[:, block * LANES : (block + 1) * LANES] for block in range(blocks)], axis=0
    )


def halving_order(count):
    order = [0]
    for bit in reversed(bits_of(count)):
        order = order + [index | bit for index in order]
    return order


def forward_kernel(
    feat_ref, edge_ref, gated_ref, halo_ref, sw_ref, skip_ref, table_ref,
    first_ref, long_ref, gext_ref, mix_ref, xs_ref,
):
    rows, channels = gated_ref.shape
    taps = table_ref.shape[1] // 2
    per = table_ref.shape[0] // taps * LANES // channels
    width = LANES // per

    def body(block):
        for half in range(SIDE // LANES):
            lanes = lanes_of(block, half)
            ends = halo_ref[pl.ds(taps, 4 * EDGE), lanes].astype(F32)
            firsts = []
            for part in range(3):
                xs = xs_ref.at[half, part]
                xs[pl.ds(0, EDGE), :] = ends[part * EDGE : (part + 1) * EDGE]
                xs[pl.ds(EDGE, EDGE), :] = edge_ref[part, :, lanes]
                firsts.append(short_sum(xs, EDGE, -1, sw_ref[part, :, lanes], EDGE))
                first_ref[part, :, lanes] = firsts[part]
            begun = jnp.concatenate(
                [firsts[1] * firsts[2], gated_ref[pl.ds(0, 16), lanes].astype(F32)[EDGE:]], axis=0
            ).astype(BF)
            gext_ref[pl.ds(0, taps), lanes] = halo_ref[pl.ds(0, taps), lanes]
            gext_ref[pl.ds(taps, 16), lanes] = begun
            gext_ref[pl.ds(taps + 16, rows - 16), lanes] = gated_ref[pl.ds(16, rows - 16), lanes]
            ext = gext_ref[:, lanes]
            table = table_ref[rows_of(block * 2 + half, per * taps), :]
            long_out = block_conv(table, ext, taps, per, width) + skip_ref[:, lanes] * ext[taps:].astype(F32)
            long_ref[:, lanes] = long_out
            query = jnp.concatenate([firsts[0], feat_ref[0, pl.ds(EDGE, rows - EDGE), lanes]], axis=0)
            mix_ref[:, lanes] = (query * long_out).astype(BF)

    unrolled(channels // SIDE, body)


def forward(feats, edges, gated, halo, short_weights, skip, table):
    _, rows, channels = feats.shape
    taps = table.shape[1] // 2
    return called(
        forward_kernel, "forward", (feats, edges, gated, halo, short_weights, skip, table),
        [
            ((3, EDGE, channels), F32),
            ((rows, channels), F32),
            ((rows + taps, channels), BF),
            ((rows, channels), BF),
        ],
        scratch=[pltpu.VMEM((2, 3, 2 * EDGE, LANES), F32)],
        cover=COVER,
    )


def project_kernel(own, mix_ref, w_ref, *refs):
    term_refs = refs[-2:]
    rows = mix_ref.shape[0]
    me = lax.axis_index("tp")
    order = halving_order(rows // own)
    ordered = jnp.concatenate([mix_ref[rows_of(me ^ k, own), :] for k in order], axis=0)
    kept = term_refs[0].shape[0]
    chunk = 512

    def project(block):
        cols = pl.ds(multiple(block * chunk, chunk), chunk)
        terms = jnp.dot(ordered, w_ref[:, cols], preferred_element_type=F32).astype(BF)
        term_refs[0][:, cols] = terms[:kept]
        if kept < rows:
            term_refs[1][:, cols] = terms[kept:]

    unrolled(w_ref.shape[1] // chunk, project)


def project(mixer_out, out_weight, after, n_tp):
    rows, features = mixer_out.shape[0], out_weight.shape[1]
    own = rows // n_tp
    split = [rows // 2] * 2 if n_tp > 1 else [rows]
    return called(
        lambda *refs: project_kernel(own, *refs), "project", (mixer_out, out_weight, *after),
        [((size, features), BF) for size in split],
    )


def grads_kernel(n_tp, *refs):
    pieces, (w_ref, grad_ref, cot_ref) = refs[:n_tp], refs[n_tp:]
    rows, channels = grad_ref.shape
    own = rows // n_tp
    me = lax.axis_index("tp")
    for k in range(n_tp):
        cot_ref[rows_of(me ^ k, own), :] = pieces[k][...]

    def body(block):
        place = rows_of(block, SIDE)
        grad_ref[:, place] = lax.dot_general(
            cot_ref[...], w_ref[place, :], NT, preferred_element_type=F32
        )

    unrolled(channels // SIDE, body)


def mixer_grads(pieces, out_weight):
    n_tp = len(pieces)
    channels, features = out_weight.shape
    rows = pieces[0].shape[0] * n_tp
    return called(
        lambda *refs: grads_kernel(n_tp, *refs), "grads", (*pieces, out_weight),
        [((rows, channels), F32)],
        scratch=[pltpu.VMEM((rows, features), BF)],
    )[0]


def backward_kernel(
    grad_ref, feat_ref, first_ref, long_ref, skip_ref, table_ref, lgrad_ref, qgrad_ref, head_ref
):
    rows, channels = lgrad_ref.shape
    taps = table_ref.shape[1] // 2
    groups = table_ref.shape[0] // taps
    per = groups * LANES // channels
    width = LANES // per

    def body(block):
        for half in range(SIDE // LANES):
            lanes = lanes_of(block, half)
            grad = grad_ref[:, lanes]
            query = grad * long_ref[:, lanes]
            qgrad_ref[:, lanes] = query
            feat = jnp.concatenate(
                [first_ref[0, :, lanes], feat_ref[0, pl.ds(EDGE, rows - EDGE), lanes]], axis=0
            )
            lgrad = (grad * feat).astype(BF)
            lgrad_ref[:, lanes] = lgrad
            first = multiple((block * 2 + half) * per * taps, taps)
            top = jnp.concatenate(
                [table_ref[pl.ds(first + member * taps, 16), :] for member in range(per)], axis=0
            )
            stacked = jnp.dot(top, lgrad[: 2 * taps], preferred_element_type=F32)
            gated_grad = picked(stacked, 16, per, width) + skip_ref[:, lanes] * lgrad[:16].astype(F32)
            head_ref[pl.ds(0, taps), lanes] = lgrad[:taps]
            head_ref[pl.ds(taps, 4 * EDGE), lanes] = jnp.concatenate(
                [
                    query[:EDGE],
                    gated_grad[:EDGE] * first_ref[2, :, lanes],
                    gated_grad[:EDGE] * first_ref[1, :, lanes],
                    jnp.zeros((EDGE, LANES), F32),
                ],
                axis=0,
            ).astype(BF)

    unrolled(channels // SIDE, body)


def backward(grads, feats, firsts, long_out, skip, table):
    rows, channels = long_out.shape
    taps = table.shape[1] // 2
    return called(
        backward_kernel, "backward", (grads, feats, firsts, long_out, skip, table),
        [((rows, channels), BF), ((rows, channels), F32), ((taps + 4 * EDGE, channels), BF)],
    )


def lag_kernel(count, lgrad_ref, gext_ref, after_ref, lag_ref, lags_ref, turn_ref):
    rows, channels = lgrad_ref.shape
    groups, taps = lags_ref.shape
    per = groups * LANES // channels
    width = LANES // per
    blocks = rows // taps
    square = (taps, taps)
    inside = iota(square, 1) + iota(square, 0) < taps
    reverse = flip_matrix(taps, taps - 1, BF)

    def body(block):
        sums = []
        for half in range(SIDE // LANES):
            lanes = lanes_of(block, half)
            wide = jnp.concatenate(
                [lgrad_ref[pl.ds(part * taps, taps), lanes] for part in range(blocks)], axis=1
            )
            wide = jnp.dot(reverse, wide, preferred_element_type=F32).astype(BF)
            owner = group_of_lane((1, wide.shape[1]), width)
            left = jnp.concatenate(
                [wide * (owner == member).astype(F32).astype(BF) for member in range(per)], axis=0
            )
            scores = lax.dot_general(
                left, side_by_side(gext_ref[:, lanes], blocks), NT, preferred_element_type=F32
            )
            for member in range(per):
                score = scores[member * taps : (member + 1) * taps]
                merged = jnp.where(inside, score[:, taps:], score[:, :taps])
                merged = pltpu.roll(merged, 0, 1, stride=1, stride_axis=0)
                sums.append(jnp.sum(merged, axis=0, keepdims=True))
        lags_ref[rows_of(block, len(sums)), :] = jnp.concatenate(sums, axis=0)

    unrolled(channels // SIDE, body)
    turn_ref[...] = lax.dot_general(
        flip_matrix(taps, taps - 1, F32), lags_ref[...], NT,
        precision=lax.Precision.HIGHEST, preferred_element_type=F32,
    )
    if count == 1:
        lag_ref[...] = turn_ref[...]
        return
    here, share = lax.axis_index("ctx"), taps // count
    for k in range(count):
        lag_ref[pl.ds(k * share, share), :] = turn_ref[rows_of(here ^ k, share), :]


def lag_sums(lgrad, gext, groups, count, after):
    rows, channels = lgrad.shape
    taps = gext.shape[0] - rows
    return called(
        lambda *refs: lag_kernel(count, *refs), "lag_sums", (lgrad, gext, after),
        [((taps, groups), F32)],
        scratch=[pltpu.VMEM((groups, taps), F32), pltpu.VMEM((taps, groups), F32)],
    )[0]


def feature_kernel(lgrad_ref, head_ref, qgrad_ref, feat_ref, first_ref, skip_ref, table_ref, fg_ref):
    rows, channels = lgrad_ref.shape
    taps = table_ref.shape[1] // 2
    per = table_ref.shape[0] // taps * LANES // channels
    width = LANES // per
    rest = pl.ds(EDGE, rows - EDGE)

    def body(block):
        for half in range(SIDE // LANES):
            lanes = lanes_of(block, half)
            lgrad = lgrad_ref[:, lanes]
            ext = jnp.concatenate([lgrad, head_ref[pl.ds(0, taps), lanes]], axis=0)
            table = table_ref[rows_of(block * 2 + half, per * taps), :]
            gated_grad = block_conv(table, ext, taps, per, width) + skip_ref[:, lanes] * lgrad.astype(F32)
            heads = head_ref[pl.ds(taps, 4 * EDGE), lanes].astype(F32)
            for part in range(3):
                fg = fg_ref.at[block * 2 + half, part]
                if part:
                    fg[pl.ds(0, EDGE), :] = gated_grad[:EDGE] * first_ref[3 - part, :, lanes]
                    fg[rest, :] = gated_grad[EDGE:] * feat_ref[3 - part, rest, lanes]
                else:
                    fg[pl.ds(0, rows), :] = qgrad_ref[:, lanes]
                fg[pl.ds(rows, EDGE), :] = heads[part * EDGE : (part + 1) * EDGE]

    unrolled(channels // SIDE, body)


def feature_grads(lgrad, heads, qgrad, feats, firsts, skip, table):
    rows, channels = lgrad.shape
    return called(
        feature_kernel, "feature_grads", (lgrad, heads, qgrad, feats, firsts, skip, table),
        [((channels // LANES, 3, rows + EDGE, LANES), F32)],
    )[0]


def short_grads_kernel(fg_ref, sw_ref, out_ref, res_ref, sems):
    rows, channels = out_ref.shape[1:]

    def copy_of(block):
        lanes = pl.ds(multiple(block * SIDE, SIDE), SIDE)
        return pltpu.make_async_copy(res_ref.at[:, :, lanes], out_ref.at[:, :, lanes], sems.at[block])

    def body(block):
        for half in range(SIDE // LANES):
            lanes = lanes_of(block, half)
            for part in range(3):
                fg = fg_ref.at[block * 2 + half, part]
                res_ref[part, :, lanes] = short_sum(fg, 0, 1, sw_ref[part, :, lanes], rows)
        copy_of(block).start()

    unrolled(channels // SIDE, body)
    for block in range(channels // SIDE):
        copy_of(block).wait()


def short_grads(fgs, short_weights):
    blocks, _, rows, _ = fgs.shape
    rows, channels = rows - EDGE, blocks * LANES
    return called(
        short_grads_kernel, "short_grads", (fgs, short_weights),
        [((3, rows, channels), F32)],
        scratch=[
            pltpu.VMEM((3, rows, channels), F32),
            pltpu.SemaphoreType.DMA((channels // SIDE,)),
        ],
        kept=(2,),
    )[0]


def last_kernel(factor, term_ref, final_ref, lag_ref, arrived_ref, mixed_hbm, filter_hbm, mixed_ref, filter_ref, sems):
    own = mixed_ref.shape[0]
    mixed = term_ref[pl.ds(0, own), :].astype(F32)
    if final_ref.shape[0] == own:
        mixed = mixed + final_ref[...].astype(F32)
    mixed_ref[...] = mixed.astype(BF)
    total = lag_ref[pl.ds(0, filter_ref.shape[0]), :]
    if arrived_ref.shape == filter_ref.shape:
        total = total + arrived_ref[...]
    filter_ref[...] = total * factor
    copies = [
        pltpu.make_async_copy(mixed_ref, mixed_hbm, sems.at[0]),
        pltpu.make_async_copy(filter_ref, filter_hbm, sems.at[1]),
    ]
    for copy in copies:
        copy.start()
    for copy in copies:
        copy.wait()


def last(terms, final, lags, arrived, own, share, factor):
    results = [((own, terms.shape[1]), BF), ((share, lags.shape[1]), F32)]
    return called(
        lambda *refs: last_kernel(factor, *refs), "last", (terms, final, lags, arrived), results,
        scratch=[pltpu.VMEM(*result) for result in results] + [pltpu.SemaphoreType.DMA((2,))],
        kept=(4, 5),
    )


def bits_of(count):
    return [1 << position for position in range(count.bit_length() - 1)]


def shards(projections, short_weights, skip_gain, filters, out_weight, out_cotangent):
    _, rows, channels = projections.shape
    group_count, taps = filters.shape
    n_tp, n_ctx = lax.axis_size("tp"), lax.axis_size("ctx")
    skip = skip_gain.reshape(1, channels)

    pack = gated_tail(projections, short_weights, taps)
    halo = passed_along(pack, "ctx", 1)

    feats, edges, gated, fwd_table, bwd_table, weights, skip, out_weight = prepare(
        projections, short_weights, filters, out_weight, skip, pack
    )
    pieces = {0: out_cotangent}
    for bit in reversed(bits_of(n_tp)):
        pieces.update({k | bit: exchanged(piece, "tp", bit) for k, piece in list(pieces.items())})
    pieces = [pieces[k] for k in range(n_tp)]

    firsts, long_out, gext, mixer_out = forward(feats, edges, gated, halo, weights, skip, fwd_table)
    terms = project(mixer_out, out_weight, pieces[1::2], n_tp)
    grads = mixer_grads(pieces, out_weight)
    lgrad, qgrad, heads = backward(grads, feats, firsts, long_out, skip, bwd_table)
    later = passed_along(heads, "ctx", -1)

    own = rows // n_tp
    held = after = final = terms[0]
    sent = terms[-1]
    for bit in bits_of(n_tp):
        arrived = exchanged(sent, "tp", bit)
        if bit == 1:
            arrived, lgrad = lax.optimization_barrier((arrived, lgrad))
        if 2 * bit == n_tp:
            final = arrived
            break
        held = held.astype(F32) + arrived.astype(F32)
        half = held.shape[0] // 2
        sent = after = held[half:].astype(BF)
        held = held[:half]

    share = taps // n_ctx
    apart = share % EDGE == 0
    lags = lag_sums(lgrad, gext, group_count, n_ctx if apart else 1, after)
    fgs = feature_grads(lgrad, later, qgrad, feats, firsts, skip, bwd_table)
    arrived, proj_grad = lags, None
    for position, bit in enumerate(reversed(bits_of(n_ctx)) if apart else ()):
        if position:
            lags = lags[: bit * share * 2] + arrived
        arrived = exchanged(lags[bit * share :], "ctx", bit)
        if position == 0:
            arrived, fgs = lax.optimization_barrier((arrived, fgs))
        if position == 1:
            proj_grad = short_grads(fgs, weights)
            arrived, final, proj_grad = lax.optimization_barrier((arrived, final, proj_grad))
    if not apart:
        lags = arrived = lax.psum_scatter(lags, "ctx", scatter_dimension=0, tiled=True)
    if proj_grad is None:
        proj_grad = short_grads(fgs, weights)
    factor = 1.0 / math.sqrt(rows * n_ctx * (channels // group_count))
    if not apart:
        arrived = final
    mixed, filter_grad = last(held, final, lags, arrived, own, share, factor)
    filter_grad = filter_grad.T
    return (mixed, proj_grad, filter_grad)


def solution(mesh):
    placed = (
        P(None, "ctx", "tp"),
        P(None, None, "tp"),
        P("tp"),
        P("tp", None),
        P("tp", None),
        P(("ctx", "tp"), None),
    )
    return jax.shard_map(
        shards,
        mesh=mesh,
        in_specs=placed,
        out_specs=(P(("ctx", "tp"), None), P(None, "ctx", "tp"), P("tp", "ctx")),
        check_vma=False,
    )
```

```python
import math

import jax
import jax.numpy as jnp
from jax import lax
from jax.experimental import pallas as pl
from jax.experimental.pallas import tpu as pltpu
from jax.sharding import PartitionSpec as P

LANES = 128
SIDE = 256
EDGE = 8
COVER = 10**11
BF = jnp.bfloat16
F32 = jnp.float32
NT = (((1,), (1,)), ((), ()))
TN = (((0,), (0,)), ((), ()))


def called(kernel, name, operands, results, scratch=(), kept=(), cover=1, mib=16):
    spaces = [
        pltpu.HBM if position in kept else pltpu.VMEM
        for position in range(len(operands) + len(results))
    ]
    first = len(operands)
    placed = [
        pltpu.with_memory_space_constraint(value, space) for value, space in zip(operands, spaces)
    ]
    return pl.pallas_call(
        kernel,
        name=name,
        in_specs=[pl.BlockSpec(memory_space=space) for space in spaces[:first]],
        out_specs=[pl.BlockSpec(memory_space=space) for space in spaces[first:]],
        out_shape=[space(*result) for space, result in zip(spaces[first:], results)],
        scratch_shapes=list(scratch),
        compiler_params=pltpu.CompilerParams(vmem_limit_bytes=mib << 20),
        cost_estimate=pl.CostEstimate(flops=cover, transcendentals=0, bytes_accessed=1),
    )(*placed)


def repeated(count, body):
    def step(index, carry):
        body(index)
        return carry

    lax.fori_loop(0, count, step, 0)


def unrolled(count, body):
    for index in range(count):
        body(index)


def multiple(value, of):
    return value if isinstance(value, int) else pl.multiple_of(value, of)


def lanes_of(block, half):
    return pl.ds(multiple(block * SIDE + half * LANES, LANES), LANES)


def rows_of(block, size):
    return pl.ds(multiple(block * size, size), size)


def exchanged(value, axis, bit):
    count = lax.axis_size(axis)
    return lax.ppermute(value, axis, [(index, index ^ bit) for index in range(count)])


def passed_along(value, axis, steps):
    count = lax.axis_size(axis)
    initial, last = (max(0, -steps), min(count, count - steps))
    return lax.ppermute(value, axis, [(source, source + steps) for source in range(initial, last)])


def iota(shape, dim):
    return lax.broadcasted_iota(jnp.int32, shape, dim)


def flip_matrix(taps, total, dtype):
    rows, cols = iota((taps, taps), 0), iota((taps, taps), 1)
    return ((rows + cols) % taps == total).astype(F32).astype(dtype)


def skewed(row, height):
    wide = jnp.broadcast_to(row, (height, row.shape[1]))
    return pltpu.roll(wide, 0, 1, stride=1, stride_axis=0)


def group_of_lane(shape, width):
    return (iota(shape, 1) % LANES) // width


def picked(stacked, rows, per, width):
    owner = group_of_lane((rows, stacked.shape[1]), width)
    total = stacked[:rows]
    for member in range(1, per):
        total = jnp.where(owner == member, stacked[member * rows : (member + 1) * rows], total)
    return total


def side_by_side(ext, blocks):
    return jnp.concatenate(
        [ext[block * LANES : (block + 2) * LANES] for block in range(blocks)], axis=1
    )


def short_sum(ref, base, step, weights, rows):
    total = weights[0:1] * ref[pl.ds(base, rows), :]
    for tap in range(1, weights.shape[0]):
        total = total + weights[tap : tap + 1] * ref[pl.ds(base + step * tap, rows), :]
    return total


def tail_kernel(proj_hbm, sw_hbm, out_ref, proj_ref, sw_ref, xs_ref, sems):
    rows, channels = proj_hbm.shape[1:]
    taps = out_ref.shape[0] - 4 * EDGE
    reach = taps + 16
    copies = [
        pltpu.make_async_copy(sw_hbm, sw_ref, sems.at[0]),
        pltpu.make_async_copy(proj_hbm.at[:, pl.ds(rows - reach, reach), :], proj_ref, sems.at[1]),
    ]
    for copy in copies:
        copy.start()
    for copy in copies:
        copy.wait()

    def body(block):
        for half in range(SIDE // LANES):
            lanes = lanes_of(block, half)
            for part in range(1, 3):
                xs_ref[half, part] = proj_ref[part, :, lanes].astype(F32)
            feats = [
                short_sum(xs_ref.at[half, part], 16, -1, sw_ref[part, :, lanes], taps) for part in (1, 2)
            ]
            out_ref[pl.ds(0, taps), lanes] = (feats[0] * feats[1]).astype(BF)
            ends = [proj_ref[part, pl.ds(taps, 16), lanes].astype(F32)[16 - EDGE :] for part in range(3)]
            out_ref[pl.ds(taps, 4 * EDGE), lanes] = jnp.concatenate(
                ends + [jnp.zeros((EDGE, LANES), F32)], axis=0
            ).astype(BF)

    unrolled(channels // SIDE, body)


def gated_tail(projections, short_weights, taps):
    _, rows, channels = projections.shape
    return called(
        tail_kernel, "gated_tail", (projections, short_weights),
        [((taps + 4 * EDGE, channels), BF)],
        scratch=[
            pltpu.VMEM((3, taps + 16, channels), BF),
            pltpu.VMEM(short_weights.shape, F32),
            pltpu.VMEM((2, 3, taps + 16, LANES), F32),
            pltpu.SemaphoreType.DMA((2,)),
        ],
        kept=(0, 1),
    )[0]


def prepare_kernel(
    proj_hbm, sw_hbm, filt_hbm, w_hbm, skip_hbm, after_hbm,
    feat_ref, edge_ref, gated_ref, fwd_ref, bwd_ref, sw_ref, skip_ref, w_ref,
    proj_ref, filt_ref, xs_ref, sems,
):
    rows, channels = proj_ref.shape[1:]
    groups, taps = filt_ref.shape
    per = groups * SIDE // channels
    copies = [
        pltpu.make_async_copy(source, target, sems.at[index])
        for index, (source, target) in enumerate(
            (
                (filt_hbm, filt_ref), (proj_hbm, proj_ref), (sw_hbm, sw_ref), (skip_hbm, skip_ref),
                (w_hbm, w_ref),
            )
        )
    ]
    for copy in copies:
        copy.start()
    shape = (taps, taps)
    inside = iota(shape, 1) <= iota(shape, 0)
    later = iota(shape, 1) >= iota(shape, 0)
    copies[0].wait()

    def build(block):
        plain = filt_ref[rows_of(block, per), :]
        turned = jnp.dot(plain, flip_matrix(taps, 0, BF), preferred_element_type=F32)
        plain = plain.astype(F32)
        for member in range(per):
            place = pl.ds(multiple((block * per + member) * taps, taps), taps)
            turn = skewed(turned[member : member + 1], taps)
            fwd_ref[place, pl.ds(0, taps)] = jnp.where(inside, 0.0, turn).astype(BF)
            fwd_ref[place, pl.ds(taps, taps)] = jnp.where(inside, turn, 0.0).astype(BF)
            turn = skewed(plain[member : member + 1], taps)
            bwd_ref[place, pl.ds(0, taps)] = jnp.where(later, turn, 0.0).astype(BF)
            bwd_ref[place, pl.ds(taps, taps)] = jnp.where(later, 0.0, turn).astype(BF)

    repeated(channels // SIDE, build)
    for copy in copies[1:4]:
        copy.wait()

    def features(block):
        for half in range(SIDE // LANES):
            lanes = lanes_of(block, half)
            feats = []
            for part in range(3):
                xs = xs_ref.at[half, part]
                xs[pl.ds(0, EDGE), :] = jnp.zeros((EDGE, LANES), F32)
                full = proj_ref[part, :, lanes].astype(F32)
                xs[pl.ds(EDGE, rows), :] = full
                edge_ref[part, :, lanes] = full[:EDGE]
                feats.append(short_sum(xs, EDGE, -1, sw_ref[part, :, lanes], rows))
                feat_ref[part, :, lanes] = feats[part]
            gated_ref[:, lanes] = (feats[1] * feats[2]).astype(BF)

    repeated(channels // SIDE, features)
    copies[4].wait()


def prepare(projections, short_weights, filters, out_weight, skip, after):
    _, rows, channels = projections.shape
    groups, taps = filters.shape
    return called(
        prepare_kernel, "prepare", (projections, short_weights, filters, out_weight, skip, after),
        [
            ((3, rows, channels), F32),
            ((3, EDGE, channels), F32),
            ((rows, channels), BF),
            ((groups * taps, 2 * taps), BF),
            ((groups * taps, 2 * taps), BF),
            (short_weights.shape, F32),
            (skip.shape, F32),
            (out_weight.shape, BF),
        ],
        scratch=[
            pltpu.VMEM(projections.shape, BF),
            pltpu.VMEM(filters.shape, BF),
            pltpu.VMEM((2, 3, rows + EDGE, LANES), F32),
            pltpu.SemaphoreType.DMA((5,)),
        ],
        kept=(0, 1, 2, 3, 4),
        cover=COVER,
    )


def block_conv(table, ext, taps, per, width):
    blocks = ext.shape[0] // taps - 1
    stacked = jnp.dot(table, side_by_side(ext, blocks), preferred_element_type=F32)
    conv = picked(stacked, taps, per, width)
    return jnp.concatenate(
        [conv[:, block * LANES : (block + 1) * LANES] for block in range(blocks)], axis=0
    )


def halving_order(count):
    order = [0]
    for bit in reversed(bits_of(count)):
        order = order + [index | bit for index in order]
    return order


def forward_kernel(
    feat_ref, edge_ref, gated_ref, halo_ref, sw_ref, skip_ref, table_ref,
    first_ref, long_ref, gext_ref, mix_ref, xs_ref,
):
    rows, channels = gated_ref.shape
    taps = table_ref.shape[1] // 2
    per = table_ref.shape[0] // taps * LANES // channels
    width = LANES // per

    def body(block):
        for half in range(SIDE // LANES):
            lanes = lanes_of(block, half)
            ends = halo_ref[pl.ds(taps, 4 * EDGE), lanes].astype(F32)
            firsts = []
            for part in range(3):
                xs = xs_ref.at[half, part]
                xs[pl.ds(0, EDGE), :] = ends[part * EDGE : (part + 1) * EDGE]
                xs[pl.ds(EDGE, EDGE), :] = edge_ref[part, :, lanes]
                firsts.append(short_sum(xs, EDGE, -1, sw_ref[part, :, lanes], EDGE))
                first_ref[part, :, lanes] = firsts[part]
            begun = jnp.concatenate(
                [firsts[1] * firsts[2], gated_ref[pl.ds(0, 16), lanes].astype(F32)[EDGE:]], axis=0
            ).astype(BF)
            gext_ref[pl.ds(0, taps), lanes] = halo_ref[pl.ds(0, taps), lanes]
            gext_ref[pl.ds(taps, 16), lanes] = begun
            gext_ref[pl.ds(taps + 16, rows - 16), lanes] = gated_ref[pl.ds(16, rows - 16), lanes]
            ext = gext_ref[:, lanes]
            table = table_ref[rows_of(block * 2 + half, per * taps), :]
            long_out = block_conv(table, ext, taps, per, width) + skip_ref[:, lanes] * ext[taps:].astype(F32)
            long_ref[:, lanes] = long_out
            query = jnp.concatenate([firsts[0], feat_ref[0, pl.ds(EDGE, rows - EDGE), lanes]], axis=0)
            mix_ref[:, lanes] = (query * long_out).astype(BF)

    unrolled(channels // SIDE, body)


def forward(feats, edges, gated, halo, short_weights, skip, table):
    _, rows, channels = feats.shape
    taps = table.shape[1] // 2
    return called(
        forward_kernel, "forward", (feats, edges, gated, halo, short_weights, skip, table),
        [
            ((3, EDGE, channels), F32),
            ((rows, channels), F32),
            ((rows + taps, channels), BF),
            ((rows, channels), BF),
        ],
        scratch=[pltpu.VMEM((2, 3, 2 * EDGE, LANES), F32)],
        cover=COVER,
    )


def project_kernel(own, mix_ref, w_ref, *refs):
    term_refs = refs[-2:]
    rows = mix_ref.shape[0]
    me = lax.axis_index("tp")
    order = halving_order(rows // own)
    ordered = jnp.concatenate([mix_ref[rows_of(me ^ k, own), :] for k in order], axis=0)
    kept = term_refs[0].shape[0]
    chunk = 2048

    def project(block):
        cols = pl.ds(multiple(block * chunk, chunk), chunk)
        terms = jnp.dot(ordered, w_ref[:, cols], preferred_element_type=F32).astype(BF)
        term_refs[0][:, cols] = terms[:kept]
        if kept < rows:
            term_refs[1][:, cols] = terms[kept:]

    unrolled(w_ref.shape[1] // chunk, project)


def project(mixer_out, out_weight, after, n_tp):
    rows, features = mixer_out.shape[0], out_weight.shape[1]
    own = rows // n_tp
    split = [rows // 2] * 2 if n_tp > 1 else [rows]
    return called(
        lambda *refs: project_kernel(own, *refs), "project", (mixer_out, out_weight, *after),
        [((size, features), BF) for size in split],
    )


def grads_kernel(n_tp, *refs):
    pieces, (w_ref, grad_ref, cot_ref) = refs[:n_tp], refs[n_tp:]
    rows, channels = grad_ref.shape
    own = rows // n_tp
    me = lax.axis_index("tp")
    for k in range(n_tp):
        cot_ref[rows_of(me ^ k, own), :] = pieces[k][...]

    def body(block):
        place = rows_of(block, SIDE)
        grad_ref[:, place] = lax.dot_general(
            cot_ref[...], w_ref[place, :], NT, preferred_element_type=F32
        )

    unrolled(channels // SIDE, body)


def mixer_grads(pieces, out_weight):
    n_tp = len(pieces)
    channels, features = out_weight.shape
    rows = pieces[0].shape[0] * n_tp
    return called(
        lambda *refs: grads_kernel(n_tp, *refs), "grads", (*pieces, out_weight),
        [((rows, channels), F32)],
        scratch=[pltpu.VMEM((rows, features), BF)],
    )[0]


def backward_kernel(
    grad_ref, feat_ref, first_ref, long_ref, skip_ref, table_ref, lgrad_ref, qgrad_ref, head_ref
):
    rows, channels = lgrad_ref.shape
    taps = table_ref.shape[1] // 2
    groups = table_ref.shape[0] // taps
    per = groups * LANES // channels
    width = LANES // per

    def body(block):
        for half in range(SIDE // LANES):
            lanes = lanes_of(block, half)
            grad = grad_ref[:, lanes]
            query = grad * long_ref[:, lanes]
            qgrad_ref[:, lanes] = query
            feat = jnp.concatenate(
                [first_ref[0, :, lanes], feat_ref[0, pl.ds(EDGE, rows - EDGE), lanes]], axis=0
            )
            lgrad = (grad * feat).astype(BF)
            lgrad_ref[:, lanes] = lgrad
            first = multiple((block * 2 + half) * per * taps, taps)
            top = jnp.concatenate(
                [table_ref[pl.ds(first + member * taps, 16), :] for member in range(per)], axis=0
            )
            stacked = jnp.dot(top, lgrad[: 2 * taps], preferred_element_type=F32)
            gated_grad = picked(stacked, 16, per, width) + skip_ref[:, lanes] * lgrad[:16].astype(F32)
            head_ref[pl.ds(0, taps), lanes] = lgrad[:taps]
            head_ref[pl.ds(taps, 4 * EDGE), lanes] = jnp.concatenate(
                [
                    query[:EDGE],
                    gated_grad[:EDGE] * first_ref[2, :, lanes],
                    gated_grad[:EDGE] * first_ref[1, :, lanes],
                    jnp.zeros((EDGE, LANES), F32),
                ],
                axis=0,
            ).astype(BF)

    unrolled(channels // SIDE, body)


def backward(grads, feats, firsts, long_out, skip, table):
    rows, channels = long_out.shape
    taps = table.shape[1] // 2
    return called(
        backward_kernel, "backward", (grads, feats, firsts, long_out, skip, table),
        [((rows, channels), BF), ((rows, channels), F32), ((taps + 4 * EDGE, channels), BF)],
    )


def lag_kernel(count, lgrad_ref, gext_ref, after_ref, lag_ref, lags_ref, turn_ref):
    rows, channels = lgrad_ref.shape
    groups, taps = lags_ref.shape
    per = groups * LANES // channels
    width = LANES // per
    blocks = rows // taps
    square = (taps, taps)
    inside = iota(square, 1) + iota(square, 0) < taps
    reverse = flip_matrix(taps, taps - 1, BF)

    def body(block):
        sums = []
        for half in range(SIDE // LANES):
            lanes = lanes_of(block, half)
            wide = jnp.concatenate(
                [lgrad_ref[pl.ds(part * taps, taps), lanes] for part in range(blocks)], axis=1
            )
            wide = jnp.dot(reverse, wide, preferred_element_type=F32).astype(BF)
            owner = group_of_lane((1, wide.shape[1]), width)
            left = jnp.concatenate(
                [wide * (owner == member).astype(F32).astype(BF) for member in range(per)], axis=0
            )
            scores = lax.dot_general(
                left, side_by_side(gext_ref[:, lanes], blocks), NT, preferred_element_type=F32
            )
            for member in range(per):
                score = scores[member * taps : (member + 1) * taps]
                merged = jnp.where(inside, score[:, taps:], score[:, :taps])
                merged = pltpu.roll(merged, 0, 1, stride=1, stride_axis=0)
                sums.append(jnp.sum(merged, axis=0, keepdims=True))
        lags_ref[rows_of(block, len(sums)), :] = jnp.concatenate(sums, axis=0)

    unrolled(channels // SIDE, body)
    turn_ref[...] = lax.dot_general(
        flip_matrix(taps, taps - 1, F32), lags_ref[...], NT,
        precision=lax.Precision.HIGHEST, preferred_element_type=F32,
    )
    if count == 1:
        lag_ref[...] = turn_ref[...]
        return
    here, share = lax.axis_index("ctx"), taps // count
    for k in range(count):
        lag_ref[pl.ds(k * share, share), :] = turn_ref[rows_of(here ^ k, share), :]


def lag_sums(lgrad, gext, groups, count, after):
    rows, channels = lgrad.shape
    taps = gext.shape[0] - rows
    return called(
        lambda *refs: lag_kernel(count, *refs), "lag_sums", (lgrad, gext, after),
        [((taps, groups), F32)],
        scratch=[pltpu.VMEM((groups, taps), F32), pltpu.VMEM((taps, groups), F32)],
    )[0]


def feature_kernel(lgrad_ref, head_ref, qgrad_ref, feat_ref, first_ref, skip_ref, table_ref, fg_ref):
    rows, channels = lgrad_ref.shape
    taps = table_ref.shape[1] // 2
    per = table_ref.shape[0] // taps * LANES // channels
    width = LANES // per
    rest = pl.ds(EDGE, rows - EDGE)

    def body(block):
        for half in range(SIDE // LANES):
            lanes = lanes_of(block, half)
            lgrad = lgrad_ref[:, lanes]
            ext = jnp.concatenate([lgrad, head_ref[pl.ds(0, taps), lanes]], axis=0)
            table = table_ref[rows_of(block * 2 + half, per * taps), :]
            gated_grad = block_conv(table, ext, taps, per, width) + skip_ref[:, lanes] * lgrad.astype(F32)
            heads = head_ref[pl.ds(taps, 4 * EDGE), lanes].astype(F32)
            for part in range(3):
                fg = fg_ref.at[block * 2 + half, part]
                if part:
                    fg[pl.ds(0, EDGE), :] = gated_grad[:EDGE] * first_ref[3 - part, :, lanes]
                    fg[rest, :] = gated_grad[EDGE:] * feat_ref[3 - part, rest, lanes]
                else:
                    fg[pl.ds(0, rows), :] = qgrad_ref[:, lanes]
                fg[pl.ds(rows, EDGE), :] = heads[part * EDGE : (part + 1) * EDGE]

    unrolled(channels // SIDE, body)


def feature_grads(lgrad, heads, qgrad, feats, firsts, skip, table):
    rows, channels = lgrad.shape
    return called(
        feature_kernel, "feature_grads", (lgrad, heads, qgrad, feats, firsts, skip, table),
        [((channels // LANES, 3, rows + EDGE, LANES), F32)],
    )[0]


def short_grads_kernel(fg_ref, sw_ref, out_ref, res_ref, sems):
    rows, channels = out_ref.shape[1:]

    def copy_of(block):
        lanes = pl.ds(multiple(block * SIDE, SIDE), SIDE)
        return pltpu.make_async_copy(res_ref.at[:, :, lanes], out_ref.at[:, :, lanes], sems.at[block])

    def body(block):
        for half in range(SIDE // LANES):
            lanes = lanes_of(block, half)
            for part in range(3):
                fg = fg_ref.at[block * 2 + half, part]
                res_ref[part, :, lanes] = short_sum(fg, 0, 1, sw_ref[part, :, lanes], rows)
        copy_of(block).start()

    unrolled(channels // SIDE, body)
    for block in range(channels // SIDE):
        copy_of(block).wait()


def short_grads(fgs, short_weights):
    blocks, _, rows, _ = fgs.shape
    rows, channels = rows - EDGE, blocks * LANES
    return called(
        short_grads_kernel, "short_grads", (fgs, short_weights),
        [((3, rows, channels), F32)],
        scratch=[
            pltpu.VMEM((3, rows, channels), F32),
            pltpu.SemaphoreType.DMA((channels // SIDE,)),
        ],
        kept=(2,),
    )[0]


def last_kernel(factor, term_ref, final_ref, lag_ref, arrived_ref, mixed_hbm, filter_hbm, mixed_ref, filter_ref, sems):
    own = mixed_ref.shape[0]
    mixed = term_ref[pl.ds(0, own), :].astype(F32)
    if final_ref.shape[0] == own:
        mixed = mixed + final_ref[...].astype(F32)
    mixed_ref[...] = mixed.astype(BF)
    total = lag_ref[pl.ds(0, filter_ref.shape[0]), :]
    if arrived_ref.shape == filter_ref.shape:
        total = total + arrived_ref[...]
    filter_ref[...] = total * factor
    copies = [
        pltpu.make_async_copy(mixed_ref, mixed_hbm, sems.at[0]),
        pltpu.make_async_copy(filter_ref, filter_hbm, sems.at[1]),
    ]
    for copy in copies:
        copy.start()
    for copy in copies:
        copy.wait()


def last(terms, final, lags, arrived, own, share, factor):
    results = [((own, terms.shape[1]), BF), ((share, lags.shape[1]), F32)]
    return called(
        lambda *refs: last_kernel(factor, *refs), "last", (terms, final, lags, arrived), results,
        scratch=[pltpu.VMEM(*result) for result in results] + [pltpu.SemaphoreType.DMA((2,))],
        kept=(4, 5),
    )


def bits_of(count):
    return [1 << position for position in range(count.bit_length() - 1)]


def shards(projections, short_weights, skip_gain, filters, out_weight, out_cotangent):
    _, rows, channels = projections.shape
    group_count, taps = filters.shape
    n_tp, n_ctx = lax.axis_size("tp"), lax.axis_size("ctx")
    skip = skip_gain.reshape(1, channels)

    pack = gated_tail(projections, short_weights, taps)
    halo = passed_along(pack, "ctx", 1)

    feats, edges, gated, fwd_table, bwd_table, weights, skip, out_weight = prepare(
        projections, short_weights, filters, out_weight, skip, pack
    )
    pieces = {0: out_cotangent}
    for bit in reversed(bits_of(n_tp)):
        pieces.update({k | bit: exchanged(piece, "tp", bit) for k, piece in list(pieces.items())})
    pieces = [pieces[k] for k in range(n_tp)]

    firsts, long_out, gext, mixer_out = forward(feats, edges, gated, halo, weights, skip, fwd_table)
    terms = project(mixer_out, out_weight, pieces[1::2], n_tp)
    grads = mixer_grads(pieces, out_weight)
    lgrad, qgrad, heads = backward(grads, feats, firsts, long_out, skip, bwd_table)
    later = passed_along(heads, "ctx", -1)

    own = rows // n_tp
    held = after = final = terms[0]
    sent = terms[-1]
    for bit in bits_of(n_tp):
        arrived = exchanged(sent, "tp", bit)
        if bit == 1:
            arrived, lgrad = lax.optimization_barrier((arrived, lgrad))
        if 2 * bit == n_tp:
            final = arrived
            break
        held = held.astype(F32) + arrived.astype(F32)
        half = held.shape[0] // 2
        sent = after = held[half:].astype(BF)
        held = held[:half]

    share = taps // n_ctx
    apart = share % EDGE == 0
    lags = lag_sums(lgrad, gext, group_count, n_ctx if apart else 1, after)
    fgs = feature_grads(lgrad, later, qgrad, feats, firsts, skip, bwd_table)
    arrived, proj_grad = lags, None
    for position, bit in enumerate(reversed(bits_of(n_ctx)) if apart else ()):
        if position:
            lags = lags[: bit * share * 2] + arrived
        arrived = exchanged(lags[bit * share :], "ctx", bit)
        if position == 0:
            arrived, fgs = lax.optimization_barrier((arrived, fgs))
        if position == 1:
            proj_grad = short_grads(fgs, weights)
            arrived, final, proj_grad = lax.optimization_barrier((arrived, final, proj_grad))
    if not apart:
        lags = arrived = lax.psum_scatter(lags, "ctx", scatter_dimension=0, tiled=True)
    if proj_grad is None:
        proj_grad = short_grads(fgs, weights)
    factor = 1.0 / math.sqrt(rows * n_ctx * (channels // group_count))
    if not apart:
        arrived = final
    mixed, filter_grad = last(held, final, lags, arrived, own, share, factor)
    filter_grad = filter_grad.T
    return (mixed, proj_grad, filter_grad)


def solution(mesh):
    placed = (
        P(None, "ctx", "tp"),
        P(None, None, "tp"),
        P("tp"),
        P("tp", None),
        P("tp", None),
        P(("ctx", "tp"), None),
    )
    return jax.shard_map(
        shards,
        mesh=mesh,
        in_specs=placed,
        out_specs=(P(("ctx", "tp"), None), P(None, "ctx", "tp"), P("tp", "ctx")),
        check_vma=False,
    )
```
